32 devices in a mesh: dom: 8 (over z, y), batch: 4 (over x, core).
Axes of the slice: x: 2, y: 2, z: 4, core: 2. Of those that a mesh axis runs over, the one named last changes fastest.
Arguments:
- signal: bfloat16 [4096, 4, 4, 256], P('dom', 'batch'), may hold values from -6 to 6
- cotangent: bfloat16 [4096, 4, 3, 256], P('dom', 'batch'), may hold values from -6 to 6
- conv_weight: bfloat16 [2, 2, 256, 256], replicated, may hold values from -0.25 to 0.25
- mix_weight: bfloat16 [3, 256, 256], replicated, may hold values from -0.21875 to 0.21875
- send_rows: int32 [64, 16], P('dom'), may hold values from 0 to 511
- send_mask: int32 [64, 16], P('dom'), may hold values 0 or 1
- tile_vals: bfloat16 [128, 128, 128], P('dom'), may hold values from -0.26953125 to 0.26953125
- tile_row: int32 [128], P('dom'), may hold values from 0 to 3
- tile_col: int32 [128], P('dom'), may hold values from 0 to 5
- tile_mask: int32 [128], P('dom'), may hold values 0 or 1
- hub_owner: int32 [8], replicated, may hold values from 0 to 7, as said below
- hub_rows: int32 [8, 16], replicated, may hold values from 0 to 511
Outputs:
- layer_out: bfloat16 [4096, 4, 3, 256], P('dom', 'batch')
- signal_grad: bfloat16 [4096, 4, 4, 256], P('dom', 'batch')
- conv_grad: float32 [2, 2, 256, 256], replicated
- mix_grad: float32 [3, 256, 256], replicated
The draws below stay inside these ranges and needn't reach their ends.
Inputs may be any that keep to these rules, and one draw needn't show every extreme that they name: `hub_owner`: each owner slot names a different partition.
All inputs are finite; a program needn't handle non-finite values. No bound on the sum of `send_mask` or of `tile_mask` on one device may be relied on, other than what follows from the above.
Results may differ from the reference program's by a relative error of at most 0.0056.
Values may be sent and summed in bfloat16 or wider, within the bound.
A program may use at most 128 MiB of HBM per device.

```python
import math
import jax
import jax.numpy as jnp
from jax import lax

C = 256
HIST = 4
NODE_DEV = 512
BLK = 128
OWNERS = 8
HUB_PER = 16
T1 = 3
TILES = 16
CAP = 16
HALO = 128
EXT = 768
NODES = 4096
BATCH = 4
N_DOM = 8


def draw_hub_owner(key, part):
    inner_key = jax.random.fold_in(key, 11)
    order_key = jax.random.fold_in(key, 23)
    middle = jax.random.permutation(inner_key, N_DOM - 2)[:OWNERS - 2].astype(jnp.int32) + 1
    ends = jnp.array([0, N_DOM - 1], dtype=jnp.int32)
    owners = jnp.concatenate([ends, middle], 0)
    order = jax.random.permutation(order_key, OWNERS)
    return owners[order].astype(jnp.int32)


def set_ends(drawn, rng, low, high):
    longest = drawn.shape.index(max(drawn.shape))
    spots = []
    for shift in (0, 1):
        where = [jax.random.randint(jax.random.fold_in(rng, axis), (), 0, length) for axis, length in enumerate(drawn.shape)]
        where[longest] = (where[longest] + shift) % drawn.shape[longest]
        spots.append(tuple(where))
    return drawn.at[spots[0]].set(low).at[spots[1]].set(high)


def levels(key, dims, split, smallest, largest):
    factor_of = 1.0
    for position, parts in split:
        draws = jax.random.uniform(jax.random.fold_in(jax.random.fold_in(key, 6), position), (parts,), jnp.float32, smallest / len(split), largest / len(split))
        factor_of = factor_of * jnp.repeat(jnp.exp(draws), dims[position] // parts).reshape((-1,) + (1,) * (len(dims) - 1 - position))
    return factor_of


def gaussian(stream_key, dims, deviation, bound, pieces=(), held_as=jnp.bfloat16):
    values = jax.random.normal(stream_key, dims, jnp.float32) * deviation
    if len(pieces) > 0:
        values = levels(stream_key, dims, pieces, -0.22, 0.18) * values
    return jnp.clip(values, min=-bound, max=bound).astype(held_as)


def setup_inputs(seed: int = 0) -> dict:
    splits = jax.random.split(jax.random.key(seed), 13)
    signal = gaussian(splits[0], (NODES, BATCH, HIST, C), 1.0, 6.0, ((0, 8), (1, 4)))
    cotangent = gaussian(splits[1], (NODES, BATCH, T1, C), 1.0, 6.0, ((0, 8), (1, 4)))
    conv_weight = gaussian(splits[2], (2, 2, C, C), (2 * C) ** -0.5, 0.25)
    mix_weight = gaussian(splits[3], (3, C, C), (3 * C) ** -0.5, 0.21875)
    send_rows = set_ends(jax.random.randint(splits[4], (N_DOM * N_DOM, CAP), 0, NODE_DEV), jax.random.fold_in(splits[4], 1), 0, NODE_DEV - 1).astype(jnp.int32)
    send_mask = set_ends((jax.random.randint(splits[5], (N_DOM * N_DOM, CAP), 0, 3) < 2).astype(jnp.int32), jax.random.fold_in(splits[5], 1), 0, 1)
    tile_vals = gaussian(splits[6], (N_DOM * TILES, BLK, BLK), 0.045, 0.26953125, ((0, 8),))
    tile_row = set_ends(jax.random.randint(splits[7], (N_DOM * TILES,), 0, NODE_DEV // BLK), jax.random.fold_in(splits[7], 1), 0, (NODE_DEV // BLK) - 1).astype(jnp.int32)
    tile_col = set_ends(jax.random.randint(splits[8], (N_DOM * TILES,), 0, EXT // BLK), jax.random.fold_in(splits[8], 1), 0, (EXT // BLK) - 1).astype(jnp.int32)
    tile_mask = set_ends((jax.random.randint(splits[9], (N_DOM * TILES,), 0, 4) < 3).astype(jnp.int32), jax.random.fold_in(splits[9], 1), 0, 1)
    hub_owner = draw_hub_owner(jax.random.fold_in(splits[12], 71), 0)
    hub_rows = set_ends(jax.random.randint(splits[11], (OWNERS, HUB_PER), 0, NODE_DEV), jax.random.fold_in(splits[11], 1), 0, NODE_DEV - 1).astype(jnp.int32)
    return dict(signal=signal, cotangent=cotangent, conv_weight=conv_weight, mix_weight=mix_weight, send_rows=send_rows, send_mask=send_mask, tile_vals=tile_vals, tile_row=tile_row, tile_col=tile_col, tile_mask=tile_mask, hub_owner=hub_owner, hub_rows=hub_rows)


highest = lax.Precision.HIGHEST

def tile_apply(ext_rows, tile_block, row_ids, col_ids, tile_keep, row_tiles):
    block_rows = tile_block.shape[1]
    features = ext_rows.shape[1]
    chosen = ext_rows.reshape(-1, block_rows, features)[col_ids]
    product = jnp.einsum('tij,tjf->tif', tile_block.astype(jnp.float32), chosen.astype(jnp.float32), precision=highest)
    product = product * tile_keep.astype(jnp.float32)[:, None, None]
    onehot = (row_ids[None, :] == jnp.arange(row_tiles, dtype=jnp.int32)[:, None]).astype(jnp.float32)
    return jnp.einsum('rt,tif->rif', onehot, product, precision=highest).reshape(row_tiles * block_rows, features)

def tile_back(own_rows, tile_block, row_ids, col_ids, tile_keep, col_tiles):
    block_rows = tile_block.shape[1]
    features = own_rows.shape[1]
    chosen = own_rows.reshape(-1, block_rows, features)[row_ids]
    product = jnp.einsum('tji,tjf->tif', tile_block.astype(jnp.float32), chosen.astype(jnp.float32), precision=highest)
    product = product * tile_keep.astype(jnp.float32)[:, None, None]
    onehot = (col_ids[None, :] == jnp.arange(col_tiles, dtype=jnp.int32)[:, None]).astype(jnp.float32)
    return jnp.einsum('ct,tif->cif', onehot, product, precision=highest).reshape(col_tiles * block_rows, features)

def device_graph(graph, device):
    send_rows, send_mask, tile_vals, tile_row, tile_col, tile_mask, hub_owner, hub_rows = graph
    sources = lax.dynamic_index_in_dim(send_rows.reshape(N_DOM, N_DOM, CAP), device, 1, keepdims=False)
    source_keep = lax.dynamic_index_in_dim(send_mask.reshape(N_DOM, N_DOM, CAP), device, 1, keepdims=False)
    halo_index = (jnp.arange(N_DOM, dtype=jnp.int32)[:, None] * NODE_DEV + sources).reshape(-1).astype(jnp.int32)
    start = (device * TILES).astype(jnp.int32)
    tiles = (lax.dynamic_slice_in_dim(tile_vals, start, TILES, 0), lax.dynamic_slice_in_dim(tile_row, start, TILES, 0), lax.dynamic_slice_in_dim(tile_col, start, TILES, 0), lax.dynamic_slice_in_dim(tile_mask, start, TILES, 0))
    return (halo_index, source_keep.reshape(-1), tiles)

def hub_index_of(graph):
    hub_owner, hub_rows = (graph[6], graph[7])
    return (hub_owner[:, None] * NODE_DEV + hub_rows).reshape(-1).astype(jnp.int32)

def spread(field, graph):
    hub_index = hub_index_of(graph)
    hubs = field[hub_index]

    def per_device(device):
        halo_index, halo_keep, tiles = device_graph(graph, device)
        own = lax.dynamic_slice_in_dim(field, (device * NODE_DEV).astype(jnp.int32), NODE_DEV, 0)
        halo = field[halo_index] * halo_keep.astype(field.dtype)[:, None]
        ext_rows = jnp.concatenate([own, halo, hubs], 0)
        return tile_apply(ext_rows, tiles[0], tiles[1], tiles[2], tiles[3], NODE_DEV // BLK)
    return lax.map(per_device, jnp.arange(N_DOM, dtype=jnp.int32)).reshape(NODES, -1)

def gather_back(field, graph):
    hub_index = hub_index_of(graph)

    def per_device(carry, device):
        halo_index, halo_keep, tiles = device_graph(graph, device)
        start = (device * NODE_DEV).astype(jnp.int32)
        own = lax.dynamic_slice_in_dim(field, start, NODE_DEV, 0)
        ext_grad = tile_back(own, tiles[0], tiles[1], tiles[2], tiles[3], EXT // BLK)
        block = lax.dynamic_slice_in_dim(carry, start, NODE_DEV, 0) + ext_grad[:NODE_DEV]
        carry = lax.dynamic_update_slice_in_dim(carry, block, start, 0)
        carry = carry.at[halo_index].add(ext_grad[NODE_DEV:NODE_DEV + HALO] * halo_keep.astype(jnp.float32)[:, None])
        carry = carry.at[hub_index].add(ext_grad[NODE_DEV + HALO:])
        return (carry, None)
    total, unused = lax.scan(per_device, jnp.zeros(field.shape, jnp.float32), jnp.arange(N_DOM, dtype=jnp.int32))
    return total

def mm(left, right):
    return jnp.dot(left, right, preferred_element_type=jnp.float32)

def one_sample(signal_s, grad_s, conv_weight, mix_weight, graph):
    earlier = signal_s[:, :-1, :].reshape(-1, C)
    later = signal_s[:, 1:, :].reshape(-1, C)
    filt = mm(earlier, conv_weight[0, 0]) + mm(later, conv_weight[0, 1])
    gate = mm(earlier, conv_weight[1, 0]) + mm(later, conv_weight[1, 1])
    tanh_filt = jnp.tanh(filt)
    sig_gate = jax.nn.sigmoid(gate)
    hidden = (tanh_filt * sig_gate).astype(jnp.bfloat16)
    hop_one = spread(hidden.reshape(NODES, T1 * C), graph).astype(jnp.bfloat16).reshape(-1, C)
    hop_two = spread(hop_one.reshape(NODES, T1 * C), graph).astype(jnp.bfloat16).reshape(-1, C)
    mixed = later.astype(jnp.float32) + mm(hidden, mix_weight[0]) + mm(hop_one, mix_weight[1]) + mm(hop_two, mix_weight[2])
    layer_out = mixed.astype(jnp.bfloat16).reshape(NODES, T1, C)
    grad_out = grad_s.reshape(-1, C)
    mix_part = jnp.stack([mm(hidden.T, grad_out), mm(hop_one.T, grad_out), mm(hop_two.T, grad_out)])
    back_two = mm(grad_out, mix_weight[2].T).astype(jnp.bfloat16)
    back_one = mm(grad_out, mix_weight[1].T) + gather_back(back_two.reshape(NODES, T1 * C), graph).reshape(-1, C)
    back_one = back_one.astype(jnp.bfloat16)
    grad_hidden = mm(grad_out, mix_weight[0].T) + gather_back(back_one.reshape(NODES, T1 * C), graph).reshape(-1, C)
    grad_filt = (grad_hidden * sig_gate * (1.0 - tanh_filt * tanh_filt)).astype(jnp.bfloat16)
    grad_gate = (grad_hidden * tanh_filt * sig_gate * (1.0 - sig_gate)).astype(jnp.bfloat16)
    conv_part = jnp.stack([jnp.stack([mm(earlier.T, grad_filt), mm(later.T, grad_filt)]), jnp.stack([mm(earlier.T, grad_gate), mm(later.T, grad_gate)])])
    into_earlier = (mm(grad_filt, conv_weight[0, 0].T) + mm(grad_gate, conv_weight[1, 0].T)).reshape(NODES, T1, C)
    into_later = (mm(grad_filt, conv_weight[0, 1].T) + mm(grad_gate, conv_weight[1, 1].T) + grad_out.astype(jnp.float32)).reshape(NODES, T1, C)
    signal_grad = jnp.pad(into_earlier, ((0, 0), (0, 1), (0, 0))) + jnp.pad(into_later, ((0, 0), (1, 0), (0, 0)))
    return (layer_out, signal_grad.astype(jnp.bfloat16), conv_part, mix_part)

def reference(signal, cotangent, conv_weight, mix_weight, send_rows, send_mask, tile_vals, tile_row, tile_col, tile_mask, hub_owner, hub_rows):
    graph = (send_rows, send_mask, tile_vals, tile_row, tile_col, tile_mask, hub_owner, hub_rows)

    def per_sample(sample_pair):
        return one_sample(sample_pair[0], sample_pair[1], conv_weight, mix_weight, graph)
    outs, grads, conv_parts, mix_parts = lax.map(per_sample, (jnp.moveaxis(signal, 1, 0), jnp.moveaxis(cotangent, 1, 0)))
    factor = 1.0 / math.sqrt(NODES * BATCH * T1)
    return (jnp.moveaxis(outs, 0, 1), jnp.moveaxis(grads, 0, 1), lax.optimization_barrier(jnp.sum(conv_parts, 0)) * factor, lax.optimization_barrier(jnp.sum(mix_parts, 0)) * factor)
```

```python
import functools
import math

import jax
import jax.numpy as jnp
import numpy as np
from jax import lax
from jax.experimental import pallas as pl
from jax.experimental.pallas import tpu as pltpu
from jax.sharding import PartitionSpec as P

VMEM = pl.BlockSpec(memory_space=pltpu.VMEM)
SMEM = pl.BlockSpec(memory_space=pltpu.SMEM)
ANY = pl.BlockSpec(memory_space=pl.ANY)
MESH = pl.DeviceIdType.MESH
F32 = jnp.float32
BF16 = jnp.bfloat16


def nn(left, right):
    return lax.dot_general(left, right, (((1,), (0,)), ((), ())), preferred_element_type=F32)


def nt(left, right):
    return lax.dot_general(left, right, (((1,), (1,)), ((), ())), preferred_element_type=F32)


def halves(size):
    return (size // 2, 2) if size % 2 == 0 else (size, 1)


def padded(rows):
    return -(-rows // 16) * 16


def build_kernel(
    outer,
    inner,
    row_ref,
    col_ref,
    keep_ref,
    tile_ref,
    owner_ref,
    rows_ref,
    flag_ref,
    hubs_ref,
    expand_ref,
    lane_ref,
    halo_ref,
    own_ref,
    own_t_ref,
    far_ref,
    far_t_ref,
    gather_ref,
    scatter_ref,
    dense_ref,
    place_ref,
):
    nodes = own_ref.shape[0]
    tiles, block, _ = tile_ref.shape
    own_tiles = nodes // block
    all_tiles = dense_ref.shape[0]
    slots = far_ref.shape[1]
    cap = rows_ref.shape[1]
    groups, hub_per = hubs_ref.shape
    halo_slots = expand_ref.shape[0]
    hub_width = gather_ref.shape[0] - halo_slots
    halo = halo_ref.shape[0]

    dense_ref[...] = jnp.zeros_like(dense_ref)
    for t in range(tiles):

        @pl.when(keep_ref[t] == 1)
        def _():
            rows = pl.ds(pl.multiple_of(row_ref[t] * block, block), block)
            dense_ref[col_ref[t], rows, :] += tile_ref[t].astype(F32)

    place_ref[:halo, :] = halo_ref[...]
    slot = lax.broadcasted_iota(jnp.int32, (hub_per, slots), 1)
    entry = lax.broadcasted_iota(jnp.int32, (hub_per, slots), 0) + halo_slots
    me = lax.axis_index("dom")
    hub = jnp.zeros((1, hub_per), F32)
    for o in range(groups):
        at = halo + o * hub_per
        owner = owner_ref[o]
        seat = lax.rem(owner, inner) * outer + lax.div(owner, inner)
        place_ref[at : at + hub_per, :] = jnp.where(
            slot == entry + seat * hub_width, 1.0, 0.0
        ).astype(BF16)
        owned = (owner == me).astype(F32)
        hub += owned * (hubs_ref[o : o + 1, :].astype(F32) + 1.0)
    far = nn(dense_ref[own_tiles].astype(BF16), place_ref[:block, :])
    for c in range(own_tiles + 1, all_tiles):
        at = (c - own_tiles) * block
        far += nn(dense_ref[c].astype(BF16), place_ref[at : at + block, :])
    far_ref[...] = far.astype(BF16)
    far_t_ref[...] = far.T.astype(BF16)
    for c in range(own_tiles):
        part = dense_ref[c]
        own_ref[:, c * block : (c + 1) * block] = part.astype(BF16)
        own_t_ref[c * block : (c + 1) * block, :] = part.T.astype(BF16)

    chosen = jnp.where(flag_ref[...] == 1, rows_ref[...].astype(F32) + 1.0, 0.0)
    spread = jnp.dot(
        expand_ref[...], chosen, precision=lax.Precision.HIGHEST, preferred_element_type=F32
    )
    from_halo = jnp.where(
        lax.broadcasted_iota(jnp.int32, (halo_slots, cap), 1) == lane_ref[...], spread, 0.0
    )
    from_hub = jnp.where(
        lax.broadcasted_iota(jnp.int32, (hub_width, hub_per), 1)
        == lax.broadcasted_iota(jnp.int32, (hub_width, hub_per), 0),
        jnp.broadcast_to(hub, (hub_width, hub_per)),
        0.0,
    )

    def picked(values):
        pick = (jnp.sum(values, axis=1, keepdims=True) + 0.5).astype(jnp.int32) - 1
        node = lax.broadcasted_iota(jnp.int32, (values.shape[0], nodes), 1)
        return jnp.where(pick == node, 1.0, 0.0)

    halo_pick, hub_pick = picked(from_halo), picked(from_hub)
    gather_ref[:halo_slots, :] = halo_pick.astype(BF16)
    gather_ref[halo_slots:, :] = hub_pick.astype(BF16)
    scatter_ref[...] = (
        jnp.concatenate([halo_pick] + [hub_pick] * outer, axis=0).T.astype(BF16)
    )


def rows_at(start, count):
    return pl.ds(pl.multiple_of(start, 16), count)


class Group:
    def __init__(self, trail, send_sem, recv_sem, sent, landed, where):
        self.send_sem, self.recv_sem = send_sem, recv_sem
        self.sent, self.landed, self.where = sent, landed, where
        trail.append(self)

    def push(self, source, target, where):
        pltpu.make_async_remote_copy(
            src_ref=source,
            dst_ref=target,
            send_sem=self.send_sem,
            recv_sem=self.recv_sem,
            device_id=where,
            device_id_type=MESH,
        ).start()

    def whole(self):
        return pltpu.make_async_remote_copy(
            src_ref=self.sent,
            dst_ref=self.landed,
            send_sem=self.send_sem,
            recv_sem=self.recv_sem,
            device_id=self.where,
            device_id_type=MESH,
        )

    def wait_recv(self):
        self.whole().wait_recv()

    def wait_send(self):
        self.whole().wait_send()


class Segment:
    def __init__(self, place, number, base, rows, refs, trail):
        self.p, self.n, self.base, self.rows, self.trail = place, number, base, rows, trail
        (self.grads, self.core_in, self.kept, self.out, self.inn, self.z_in, self.result) = refs[:7]
        self.send_sem, self.recv_sem = refs[7:]
        p = place
        self.half = rows // p.K
        self.piece = self.half // len(p.square)
        self.half_at = base // p.K
        self.piece_at = base // (p.K * len(p.square))
        self.mine = base + p.k * self.half + p.g * self.piece
        self.small = pl.ds(self.piece_at, self.piece)

    def group(self, stage, sent, landed, where):
        return Group(
            self.trail,
            self.send_sem.at[self.n, stage],
            self.recv_sem.at[self.n, stage],
            sent,
            landed,
            where,
        )

    def core_send(self):
        p = self.p
        if p.K == 1:
            return
        spot = self.core_in.at[pl.ds(self.half_at, self.half)]
        self.core = self.group(0, spot, spot, p.partner)
        give = self.base + p.other_k * self.half
        self.core.push(self.grads.at[rows_at(give, self.half)], spot, p.partner)

    def core_take(self):
        p = self.p
        value = self.grads[rows_at(self.base + p.k * self.half, self.half), :]
        if p.K > 1:
            self.core.wait_recv()
            value = value + self.core_in[pl.ds(self.half_at, self.half), :]
        self.kept[pl.ds(self.half_at, self.half), :] = value
        count = len(p.square)
        for g in range(count):
            self.out[g, self.small, :] = value[g * self.piece : (g + 1) * self.piece].astype(BF16)
        if count > 1:
            some = self.inn.at[pl.ds(0, count - 1), self.small]
            self.square = self.group(1, some, some, p.square_peers[0][1])
            for other, where in p.square_peers:
                self.square.push(
                    self.out.at[other, self.small], self.inn.at[p.g, self.small], where
                )

    def square_take(self):
        p = self.p
        value = self.kept[rows_at(self.half_at + p.g * self.piece, self.piece), :]
        if len(p.square) > 1:
            self.square.wait_recv()
            for other, _ in p.square_peers:
                value = value + self.inn[other, self.small, :].astype(F32)
        self.z_in[p.z, self.small, :] = value.astype(BF16)
        if p.Z > 1:
            some = self.z_in.at[pl.ds(0, p.Z - 1), self.small]
            self.line = self.group(2, some, some, p.z_peers[0][1])
            spot = self.z_in.at[p.z, self.small]
            for _, where in p.z_peers:
                self.line.push(spot, spot, where)

    def line_take(self, factor):
        p = self.p
        if p.Z > 1:
            self.line.wait_recv()
        value = self.z_in[0, self.small, :].astype(F32)
        for i in range(1, p.Z):
            value = value + self.z_in[i, self.small, :].astype(F32)
        spot = rows_at(self.mine, self.piece)
        self.result[spot, :] = (value * factor).astype(BF16)
        count = len(p.square)
        if count > 1:
            some = self.result.at[pl.ds(self.base, (count - 1) * self.piece)]
            self.spread = self.group(3, some, some, p.square_peers[0][1])
            for _, where in p.square_peers:
                self.spread.push(self.result.at[spot], self.result.at[spot], where)

    def spread_take(self):
        p = self.p
        if len(p.square) > 1:
            self.spread.wait_recv()
        if p.K > 1:
            spot = self.result.at[rows_at(self.base + p.k * self.half, self.half)]
            self.last = self.group(4, spot, spot, p.partner)
            self.last.push(spot, spot, p.partner)

    def finish(self):
        if self.p.K > 1:
            self.last.wait_recv()


class Place:
    def __init__(self, n_dom, n_batch):
        self.D = n_dom
        self.Z, self.Y = halves(n_dom)
        self.X, self.K = halves(n_batch)
        self.me = lax.axis_index("dom")
        batch = lax.axis_index("batch")
        self.z, self.y = lax.div(self.me, self.Y), lax.rem(self.me, self.Y)
        self.x, self.k = lax.div(batch, self.K), lax.rem(batch, self.K)
        self.other_k = lax.rem(self.k + 1, self.K)
        self.partner = {"batch": self.x * self.K + self.other_k}
        self.dom_peers = [lax.rem(self.me + d, n_dom) for d in range(1, n_dom)]
        self.z_peers = []
        for d in range(1, self.Z):
            seat = lax.rem(self.z + d, self.Z)
            self.z_peers.append((seat, {"dom": seat * self.Y + self.y}))
        self.y_peers = []
        for d in range(1, self.Y):
            seat = lax.rem(self.y + d, self.Y)
            self.y_peers.append((seat, {"dom": self.z * self.Y + seat}))
        self.square = range(self.X * self.Y)
        self.g = self.x * self.Y + self.y
        self.square_peers = []
        for d in range(1, self.X * self.Y):
            seat = lax.rem(self.g + d, self.X * self.Y)
            where = {
                "batch": lax.div(seat, self.Y) * self.K + self.k,
                "dom": self.z * self.Y + lax.rem(seat, self.Y),
            }
            self.square_peers.append((seat, where))

    def greet(self):
        barrier = pltpu.get_barrier_semaphore()
        peers = [{"dom": other} for other in self.dom_peers]
        if self.K > 1:
            peers.append(self.partner)
        for x in range(1, self.X):
            for y in range(self.Y):
                peers.append(
                    {
                        "batch": lax.rem(self.x + x, self.X) * self.K + self.k,
                        "dom": self.z * self.Y + lax.rem(self.y + y, self.Y),
                    }
                )
        for where in peers:
            pl.semaphore_signal(barrier, inc=1, device_id=where, device_id_type=MESH)
        return lambda: pl.semaphore_wait(barrier, len(peers))


def main_kernel(
    n_dom,
    n_batch,
    hub_w,
    factor,
    sig_ref,
    cot_ref,
    conv_ref,
    mix_ref,
    own_ref,
    own_t_ref,
    far_ref,
    far_t_ref,
    gather_ref,
    scatter_ref,
    layer_ref,
    sgrad_ref,
    result_ref,
    wide_ref,
    wide_t_ref,
    cot_t_ref,
    taps_ref,
    hidden_ref,
    hop_ref,
    back_ref,
    back_one_ref,
    slope_filt,
    slope_gate,
    hop_sum,
    back_sum,
    held_ref,
    sgrad_wide,
    grads_ref,
    out_b,
    hub_b,
    hub_in,
    hub_out,
    in_b,
    out_f,
    in_f,
    core_in,
    kept,
    square_out,
    square_in,
    z_in,
    halo_send,
    halo_recv,
    hub_send,
    hub_recv,
    seg_send,
    seg_recv,
):
    steps, nodes, chans = cot_ref.shape
    p = Place(n_dom, n_batch)
    D, Z, Y = p.D, p.Z, p.Y
    ready = p.greet()
    halo = gather_ref.shape[0] - hub_w
    hw = halo // D
    trail = []
    span = [slice(t * chans, (t + 1) * chans) for t in range(steps + 1)]
    pair = [slice(t * chans, (t + 2) * chans) for t in range(steps)]

    def group(sems, e, kind, t, sent, landed, where):
        return Group(
            trail, sems[0].at[e, kind, t], sems[1].at[e, kind, t], sent, landed, where
        )

    halo_sems, hub_sems = (halo_send, halo_recv), (hub_send, hub_recv)
    groups = {}

    def send_halo(e, kind, t):
        out, inn = (out_b, in_b) if kind == 0 else (out_f, in_f)
        some = inn.at[e, t, pl.ds(0, (D - 1) * hw)]
        g = group(halo_sems, e, kind, t, some, some, {"dom": p.dom_peers[0]})
        mine = rows_at(p.me * hw, hw)
        for other in p.dom_peers:
            g.push(
                out.at[e, t, rows_at(other * hw, hw)], inn.at[e, t, mine], {"dom": other}
            )
        groups["halo", e, kind, t] = g
        inn[e, t, mine, :] = out[e, t, mine, :]

    def send_hub_b(e, t):
        if Y == 1:
            return
        g = group(hub_sems, e, 0, t, hub_in.at[e, t], hub_in.at[e, t], p.y_peers[0][1])
        for seat, where in p.y_peers:
            g.push(
                out_b.at[e, t, rows_at(halo + seat * (Z * hub_w), Z * hub_w)],
                hub_in.at[e, t],
                where,
            )
        groups["hub", e, 0, t] = g

    def turn_hub_b(e, t):
        value = hub_b[e, t, rows_at(p.y * (Z * hub_w), Z * hub_w), :]
        if Y > 1:
            groups["hub", e, 0, t].wait_recv()
            value = value + hub_in[e, t].astype(F32)
        hub_out[e, t] = value.astype(BF16)
        mine = rows_at(halo + p.z * hub_w, hub_w)
        if Z > 1:
            some = in_b.at[e, t, pl.ds(halo, (Z - 1) * hub_w)]
            g = group(hub_sems, e, 1, t, some, some, p.z_peers[0][1])
            for seat, where in p.z_peers:
                g.push(hub_out.at[e, t, rows_at(seat * hub_w, hub_w)], in_b.at[e, t, mine], where)
            groups["hub", e, 1, t] = g
        in_b[e, t, mine, :] = hub_out[e, t, rows_at(p.z * hub_w, hub_w), :]

    def take_b(e, t):
        if D > 1:
            groups["halo", e, 0, t].wait_recv()
        if Z > 1:
            groups["hub", e, 1, t].wait_recv()
        return nn(scatter_ref[...], in_b[e, t])

    def send_hub_f(e, t):
        mine = rows_at(halo + (p.y * Z + p.z) * hub_w, hub_w)
        if Z > 1:
            some = in_f.at[e, t, pl.ds(halo, (Z - 1) * hub_w)]
            g = group(hub_sems, e, 2, t, some, some, p.z_peers[0][1])
            for _, where in p.z_peers:
                g.push(out_f.at[e, t, pl.ds(halo, hub_w)], in_f.at[e, t, mine], where)
            groups["hub", e, 2, t] = g
        in_f[e, t, mine, :] = out_f[e, t, halo:, :]

    def turn_hub_f(e, t):
        if Z > 1:
            groups["hub", e, 2, t].wait_recv()
        if Y > 1:
            column = in_f.at[e, t, rows_at(halo + p.y * (Z * hub_w), Z * hub_w)]
            g = group(hub_sems, e, 3, t, column, column, p.y_peers[0][1])
            for _, where in p.y_peers:
                g.push(column, column, where)
            groups["hub", e, 3, t] = g

    def take_f(e, t):
        if D > 1:
            groups["halo", e, 1, t].wait_recv()
        if Y > 1:
            groups["hub", e, 3, t].wait_recv()
        return nn(far_ref[...], in_f[e, t])

    def put_b(e, t, field):
        value = nn(far_t_ref[...], field)
        out_b[e, t] = value.astype(BF16)
        hub_b[e, t] = value[halo:]

    def segment(number, base, rows):
        refs = (
            grads_ref,
            core_in,
            kept,
            square_out,
            square_in,
            z_in,
            result_ref,
            seg_send,
            seg_recv,
        )
        return Segment(p, number, base * chans, rows * chans, refs, trail)

    filt_seg, gate_seg, mix_seg, last_seg = (
        segment(0, 0, 2),
        segment(1, 2, 2),
        segment(2, 4, 2),
        segment(3, 6, 1),
    )

    for t in range(steps):
        back = nt(cot_ref[t], mix_ref[2]).astype(BF16)
        back_ref[t] = back
        put_b(0, t, back)
    ready()
    for t in range(steps):
        send_hub_b(0, t)
    for t in range(steps):
        send_halo(0, 0, t)

    wide_ref[...] = sig_ref[...].reshape(nodes, (steps + 1) * chans)
    for kind in range(2):
        for tap in range(2):
            taps_ref[span[tap], span[kind]] = conv_ref[kind, tap]
    edge = nn(gather_ref[...], wide_ref[...]).astype(BF16)
    for t in range(steps):
        both = nn(edge[:, pair[t]], taps_ref[...])
        out_f[0, t] = (jnp.tanh(both[:, :chans]) * jax.nn.sigmoid(both[:, chans:])).astype(BF16)
    for t in range(steps):
        turn_hub_b(0, t)
    for t in range(steps):
        send_hub_f(0, t)
    for t in range(steps):
        send_halo(0, 1, t)

    for t in range(steps):
        back_sum[t] = nt(cot_ref[t], mix_ref[1]) + nn(own_t_ref[...], back_ref[t])
    for t in range(steps):
        both = nn(wide_ref[:, pair[t]], taps_ref[...])
        tanh_filt = jnp.tanh(both[:, :chans])
        sig_gate = jax.nn.sigmoid(both[:, chans:])
        hidden_ref[t] = (tanh_filt * sig_gate).astype(BF16)
        slope_filt[t] = sig_gate * (1.0 - tanh_filt * tanh_filt)
        slope_gate[t] = tanh_filt * sig_gate * (1.0 - sig_gate)
    for t in range(steps):
        turn_hub_f(0, t)

    for t in range(steps):
        back = (back_sum[t] + take_b(0, t)).astype(BF16)
        back_one_ref[t] = back
        put_b(1, t, back)
        send_hub_b(1, t)
        send_halo(1, 0, t)
    for t in range(steps):
        hop_sum[t] = nn(own_ref[...], hidden_ref[t])
    for t in range(steps):
        turn_hub_b(1, t)

    for t in range(steps):
        hop = (hop_sum[t] + take_f(0, t)).astype(BF16)
        hop_ref[t] = hop
        out_f[1, t] = nn(gather_ref[...], hop).astype(BF16)
        send_hub_f(1, t)
        send_halo(1, 1, t)

    wide_t_ref[...] = wide_ref[...].T
    for t in range(steps):
        back_sum[t] = nt(cot_ref[t], mix_ref[0]) + nn(own_t_ref[...], back_one_ref[t])
    for t in range(steps):
        turn_hub_f(1, t)

    for t in range(steps):
        grad_hidden = back_sum[t] + take_b(1, t)
        held_ref[t, :, :chans] = (grad_hidden * slope_filt[t]).astype(BF16)
        held_ref[t, :, chans:] = (grad_hidden * slope_gate[t]).astype(BF16)
    for kind, seg in enumerate((filt_seg, gate_seg)):
        outer = nn(wide_t_ref[pair[0], :], held_ref[0, :, span[kind]])
        for t in range(1, steps):
            outer += nn(wide_t_ref[pair[t], :], held_ref[t, :, span[kind]])
        grads_ref[kind * 2 * chans : (kind + 1) * 2 * chans, :] = outer
        seg.core_send()
    for t in range(steps):
        cot_t_ref[t] = cot_ref[t].T
    for spot, field in enumerate((hidden_ref, hop_ref)):
        part = nn(cot_t_ref[0], field[0])
        for t in range(1, steps):
            part += nn(cot_t_ref[t], field[t])
        grads_ref[(4 + spot) * chans : (5 + spot) * chans, :] = part.T
    filt_seg.core_take()
    gate_seg.core_take()
    mix_seg.core_send()

    for t in range(steps):
        hop_sum[t] = nn(own_ref[...], hop_ref[t])
    mix_seg.core_take()
    part = None
    for t in range(steps):
        hop = (hop_sum[t] + take_f(1, t)).astype(BF16)
        hop_sum[t] = nn(hop, mix_ref[2])
        here = nn(cot_t_ref[t], hop)
        part = here if part is None else part + here
    grads_ref[6 * chans :, :] = part.T
    last_seg.core_send()
    filt_seg.square_take()
    gate_seg.square_take()
    last_seg.core_take()
    mix_seg.square_take()
    for t in range(steps):
        layer_ref[t] = (
            wide_ref[:, span[t + 1]].astype(F32)
            + nn(hidden_ref[t], mix_ref[0])
            + nn(hop_ref[t], mix_ref[1])
            + hop_sum[t]
        ).astype(BF16)
    last_seg.square_take()
    carried = None
    for t in range(steps):
        into = nt(held_ref[t], taps_ref[...])
        before = into[:, :chans]
        if t > 0:
            before = before + carried
        sgrad_wide[:, span[t]] = before.astype(BF16)
        carried = into[:, chans:] + cot_ref[t].astype(F32)
    sgrad_wide[:, span[steps]] = carried.astype(BF16)
    sgrad_ref[...] = sgrad_wide[...].reshape(sgrad_ref.shape)
    order = (filt_seg, gate_seg, mix_seg, last_seg)
    for seg in order:
        seg.line_take(factor)
    for seg in order:
        seg.spread_take()
    for seg in order:
        seg.finish()
    for g in trail:
        g.wait_send()


def finish_kernel(layer_ref, sgrad_ref, result_ref, layer_out, sgrad_out, conv_out, mix_out, sems):
    copies = [
        pltpu.make_async_copy(layer_ref, layer_out, sems.at[0]),
        pltpu.make_async_copy(sgrad_ref, sgrad_out, sems.at[1]),
    ]
    for copy in copies:
        copy.start()
    rows = conv_out.shape[0]
    conv_out[...] = result_ref[:rows, :].astype(F32)
    mix_out[...] = result_ref[rows:, :].astype(F32)
    for copy in copies:
        copy.wait()


def shape_of(*dims, dtype=BF16):
    return jax.ShapeDtypeStruct(dims, dtype)


def body(
    axis_sizes,
    signal,
    cotangent,
    conv_weight,
    mix_weight,
    send_rows,
    send_mask,
    tile_vals,
    tile_row,
    tile_col,
    tile_mask,
    hub_owner,
    hub_rows,
):
    nodes, b_dev, hist, chans = signal.shape
    steps = hist - 1
    n_dom, cap = send_rows.shape
    n_batch = dict(axis_sizes)["batch"]
    outer, inner = halves(n_dom)
    square = halves(n_batch)[0] * inner
    pair = halves(n_batch)[1]
    hub_per = hub_rows.shape[1]
    hw, hub_w = padded(cap), padded(hub_per)
    halo = n_dom * hw
    slots = halo + n_dom * hub_w
    back_rows = halo + outer * hub_w
    lead_rows = halo + hub_w
    block = tile_vals.shape[1]
    entries = n_dom * cap + hub_rows.size
    all_tiles = (nodes + entries) // block

    sig = signal.reshape(nodes, hist, chans)
    cot = jnp.transpose(cotangent.reshape(nodes, steps, chans), (1, 0, 2))

    slot = np.arange(halo)
    expand = (slot[:, None] // hw == np.arange(n_dom)[None, :]).astype(np.float32)
    lane = (slot % hw).astype(np.int32)[:, None]
    entry = np.arange(n_dom * cap)
    halo_place = jnp.asarray(
        (entry // cap * hw + entry % cap)[:, None] == np.arange(slots)[None, :], dtype=BF16
    )

    mats = pl.pallas_call(
        functools.partial(build_kernel, outer, inner),
        out_shape=(
            shape_of(nodes, nodes),
            shape_of(nodes, nodes),
            shape_of(nodes, slots),
            shape_of(slots, nodes),
            shape_of(lead_rows, nodes),
            shape_of(nodes, back_rows),
        ),
        in_specs=[SMEM] * 3 + [VMEM] + [SMEM] + [VMEM] * 6,
        out_specs=(VMEM,) * 6,
        scratch_shapes=[
            pltpu.VMEM((all_tiles, nodes, block), F32),
            pltpu.VMEM((entries, slots), BF16),
        ],
        name="build",
    )(
        tile_row,
        tile_col,
        tile_mask,
        tile_vals,
        hub_owner,
        send_rows,
        send_mask,
        hub_rows,
        expand,
        lane,
        halo_place,
    )

    total_count = nodes * steps * b_dev
    for _, size in axis_sizes:
        total_count *= size
    weights = 7 * chans
    field = pltpu.VMEM((steps, nodes, chans), BF16)
    total = pltpu.VMEM((steps, nodes, chans), F32)
    wide = pltpu.VMEM((nodes, hist * chans), BF16)
    halo_sems = pltpu.SemaphoreType.DMA((2, 2, steps))
    hub_sems = pltpu.SemaphoreType.DMA((2, 4, steps))
    seg_sems = pltpu.SemaphoreType.DMA((4, 5))
    layer, sgrad, result = pl.pallas_call(
        functools.partial(
            main_kernel, n_dom, n_batch, hub_w, 1.0 / math.sqrt(total_count)
        ),
        out_shape=(
            shape_of(steps, nodes, chans),
            shape_of(nodes, hist, chans),
            shape_of(weights, chans),
        ),
        in_specs=[VMEM] * 10,
        out_specs=(VMEM,) * 3,
        scratch_shapes=[
            wide,
            pltpu.VMEM((hist * chans, nodes), BF16),
            pltpu.VMEM((steps, chans, nodes), BF16),
            pltpu.VMEM((2 * chans, 2 * chans), BF16),
            field,
            field,
            field,
            field,
            total,
            total,
            total,
            total,
            pltpu.VMEM((steps, nodes, 2 * chans), BF16),
            wide,
            pltpu.VMEM((weights, chans), F32),
            pltpu.VMEM((2, steps, slots, chans), BF16),
            pltpu.VMEM((2, steps, n_dom * hub_w, chans), F32),
            pltpu.VMEM((2, steps, outer * hub_w, chans), BF16),
            pltpu.VMEM((2, steps, outer * hub_w, chans), BF16),
            pltpu.VMEM((2, steps, back_rows, chans), BF16),
            pltpu.VMEM((2, steps, lead_rows, chans), BF16),
            pltpu.VMEM((2, steps, slots, chans), BF16),
            pltpu.VMEM((weights // pair, chans), F32),
            pltpu.VMEM((weights // pair, chans), F32),
            pltpu.VMEM((square, weights // (pair * square), chans), BF16),
            pltpu.VMEM((square, weights // (pair * square), chans), BF16),
            pltpu.VMEM((outer, weights // (pair * square), chans), BF16),
            halo_sems,
            halo_sems,
            hub_sems,
            hub_sems,
            seg_sems,
            seg_sems,
        ],
        compiler_params=pltpu.CompilerParams(collective_id=0, has_side_effects=True),
        name="main",
    )(sig, cot, conv_weight, mix_weight, *mats)

    layer_out, signal_grad, conv_grad, mix_grad = pl.pallas_call(
        finish_kernel,
        out_shape=(
            shape_of(steps, nodes, chans),
            shape_of(nodes, hist, chans),
            shape_of(4 * chans, chans, dtype=F32),
            shape_of(3 * chans, chans, dtype=F32),
        ),
        in_specs=[VMEM] * 3,
        out_specs=(ANY, ANY, VMEM, VMEM),
        scratch_shapes=[pltpu.SemaphoreType.DMA((2,))],
        name="finish",
    )(layer, sgrad, result)
    return (
        jnp.transpose(layer_out, (1, 0, 2)).reshape(nodes, b_dev, steps, chans),
        signal_grad.reshape(signal.shape),
        conv_grad.reshape(conv_weight.shape),
        mix_grad.reshape(mix_weight.shape),
    )


def solution(mesh):
    placed = (
        P("dom", "batch", None, None),
        P("dom", "batch", None, None),
        P(),
        P(),
        P("dom", None),
        P("dom", None),
        P("dom", None, None),
        P("dom"),
        P("dom"),
        P("dom"),
        P(),
        P(),
    )
    axis_sizes = tuple((axis, mesh.shape[axis]) for axis in ("dom", "batch"))
    return jax.shard_map(
        functools.partial(body, axis_sizes),
        mesh=mesh,
        in_specs=placed,
        out_specs=(P("dom", "batch", None, None), P("dom", "batch", None, None), P(), P()),
        check_vma=False,
    )
```

```python
import functools
import math

import jax
import jax.numpy as jnp
from jax import lax
from jax.experimental import pallas as pl
from jax.experimental.pallas import tpu as pltpu
from jax.sharding import PartitionSpec as P

VMEM = pl.BlockSpec(memory_space=pltpu.VMEM)
ANY = pl.BlockSpec(memory_space=pl.ANY)
HBM = pl.BlockSpec(memory_space=pltpu.HBM)
MESH = pl.DeviceIdType.MESH
BUILD_ROOM = 52 << 20
F32 = jnp.float32
BF16 = jnp.bfloat16


def nn(left, right):
    return lax.dot_general(left, right, (((1,), (0,)), ((), ())), preferred_element_type=F32)


def nt(left, right):
    return lax.dot_general(left, right, (((1,), (1,)), ((), ())), preferred_element_type=F32)


def halves(size):
    return (size // 2, 2) if size % 2 == 0 else (size, 1)


def flipped(index, size):
    total, low, high = 0, 1, size // 2
    while high >= 1:
        total = total + lax.rem(lax.div(index, low), 2) * high
        low, high = low * 2, high // 2
    return total


def padded(rows):
    return -(-rows // 16) * 16


def build_kernel(
    outer,
    inner,
    n_dom,
    hub_width,
    cap,
    hub_per,
    table_any,
    tile_any,
    own_ref,
    own_t_ref,
    far_ref,
    far_t_ref,
    gather_ref,
    scatter_ref,
    dense_ref,
    place_ref,
    ints_ref,
    table_ref,
    tile_ref,
    sems,
):
    loads = [
        pltpu.make_async_copy(source, target, sems.at[i])
        for i, (source, target) in enumerate(
            (
                (table_any, ints_ref),
                (table_any, table_ref),
                (tile_any, tile_ref),
            )
        )
    ]
    for load in loads:
        load.start()
    nodes = own_ref.shape[0]
    tiles, block, _ = tile_ref.shape
    own_tiles = nodes // block
    all_tiles = dense_ref.shape[0]
    slots = far_ref.shape[1]
    groups = ints_ref.shape[0] - 4 - 2 * n_dom
    rows_ref, flag_ref = table_ref.at[4 : 4 + n_dom], table_ref.at[4 + n_dom : 4 + 2 * n_dom]
    hubs_ref = table_ref.at[4 + 2 * n_dom :]
    halo_slots = gather_ref.shape[0] - hub_width
    halo_width = halo_slots // n_dom
    halo = n_dom * cap

    dense_ref[...] = jnp.zeros_like(dense_ref)
    entry = lax.broadcasted_iota(jnp.int32, (halo, slots), 0)
    if cap != halo_width:
        entry = lax.div(entry, cap) * halo_width + lax.rem(entry, cap)
    place_ref[:halo, :] = jnp.where(
        entry == lax.broadcasted_iota(jnp.int32, (halo, slots), 1), 1.0, 0.0
    ).astype(BF16)
    source = lax.div(lax.broadcasted_iota(jnp.int32, (halo_slots, n_dom), 0), halo_width)
    expand = (source == lax.broadcasted_iota(jnp.int32, (halo_slots, n_dom), 1)).astype(F32)
    lane = lax.rem(lax.broadcasted_iota(jnp.int32, (halo_slots, cap), 0), halo_width)
    for load in loads:
        load.wait()
    for t in range(tiles):

        @pl.when(ints_ref[2, t] == 1)
        def _():
            rows = pl.ds(pl.multiple_of(ints_ref[0, t] * block, block), block)
            dense_ref[ints_ref[1, t], rows, :] += tile_ref[t].astype(F32)

    slot = lax.broadcasted_iota(jnp.int32, (hub_per, slots), 1)
    entry = lax.broadcasted_iota(jnp.int32, (hub_per, slots), 0) + halo_slots
    me = lax.axis_index("dom")
    hub = jnp.zeros((1, hub_per), F32)
    for o in range(groups):
        at = halo + o * hub_per
        owner = ints_ref[3, o]
        seat = lax.rem(owner, inner) * outer + flipped(lax.div(owner, inner), outer)
        place_ref[at : at + hub_per, :] = jnp.where(
            slot == entry + seat * hub_width, 1.0, 0.0
        ).astype(BF16)
        owned = (owner == me).astype(F32)
        hub += owned * (hubs_ref[o : o + 1, :hub_per].astype(F32) + 1.0)
    far = nn(dense_ref[own_tiles].astype(BF16), place_ref[:block, :])
    for c in range(own_tiles + 1, all_tiles):
        at = (c - own_tiles) * block
        far += nn(dense_ref[c].astype(BF16), place_ref[at : at + block, :])
    far_ref[...] = far.astype(BF16)
    far_t_ref[...] = far.T.astype(BF16)
    for c in range(own_tiles):
        part = dense_ref[c]
        own_ref[:, c * block : (c + 1) * block] = part.astype(BF16)
        own_t_ref[c * block : (c + 1) * block, :] = part.T.astype(BF16)

    chosen = jnp.where(flag_ref[:, :cap] == 1, rows_ref[:, :cap].astype(F32) + 1.0, 0.0)
    spread = jnp.dot(
        expand, chosen, precision=lax.Precision.HIGHEST, preferred_element_type=F32
    )
    from_halo = jnp.where(
        lax.broadcasted_iota(jnp.int32, (halo_slots, cap), 1) == lane, spread, 0.0
    )
    from_hub = jnp.where(
        lax.broadcasted_iota(jnp.int32, (hub_width, hub_per), 1)
        == lax.broadcasted_iota(jnp.int32, (hub_width, hub_per), 0),
        jnp.broadcast_to(hub, (hub_width, hub_per)),
        0.0,
    )

    def picked(values):
        pick = (jnp.sum(values, axis=1, keepdims=True) + 0.5).astype(jnp.int32) - 1
        node = lax.broadcasted_iota(jnp.int32, (values.shape[0], nodes), 1)
        return jnp.where(pick == node, 1.0, 0.0)

    halo_pick, hub_pick = picked(from_halo), picked(from_hub)
    gather_ref[:halo_slots, :] = halo_pick.astype(BF16)
    gather_ref[halo_slots:, :] = hub_pick.astype(BF16)
    scatter_ref[...] = (
        jnp.concatenate([halo_pick] + [hub_pick] * min(outer, 2), axis=0).T.astype(BF16)
    )


def rows_at(start, count):
    return pl.ds(pl.multiple_of(start, 16), count)


class Group:
    def __init__(self, trail, send_sem, recv_sem, sent, landed, where):
        self.send_sem, self.recv_sem = send_sem, recv_sem
        self.sent, self.landed, self.where = sent, landed, where
        trail.append(self)

    def push(self, source, target, where):
        pltpu.make_async_remote_copy(
            src_ref=source,
            dst_ref=target,
            send_sem=self.send_sem,
            recv_sem=self.recv_sem,
            device_id=where,
            device_id_type=MESH,
        ).start()

    def whole(self):
        return pltpu.make_async_remote_copy(
            src_ref=self.sent,
            dst_ref=self.landed,
            send_sem=self.send_sem,
            recv_sem=self.recv_sem,
            device_id=self.where,
            device_id_type=MESH,
        )

    def wait_recv(self):
        self.whole().wait_recv()

    def wait_send(self):
        self.whole().wait_send()


class Segment:
    def __init__(self, place, number, base, rows, refs, trail):
        self.p, self.n, self.base, self.rows, self.trail = place, number, base, rows, trail
        (self.grads, self.core_in, self.kept, self.out, self.inn, self.z_in, self.result) = refs[:7]
        self.send_sem, self.recv_sem = refs[7:]
        p = place
        self.half = rows // p.K
        self.piece = self.half // len(p.square)
        self.half_at = base // p.K
        self.piece_at = base // (p.K * len(p.square))
        self.mine = base + p.k * self.half + p.g * self.piece
        self.small = pl.ds(self.piece_at, self.piece)

    def group(self, stage, sent, landed, where):
        return Group(
            self.trail,
            self.send_sem.at[self.n, stage],
            self.recv_sem.at[self.n, stage],
            sent,
            landed,
            where,
        )

    def core_send(self):
        p = self.p
        if p.K == 1:
            return
        spot = self.core_in.at[pl.ds(self.half_at, self.half)]
        self.core = self.group(0, spot, spot, p.partner)
        give = self.base + p.other_k * self.half
        self.core.push(self.grads.at[rows_at(give, self.half)], spot, p.partner)

    def core_take(self):
        p = self.p
        value = self.grads[rows_at(self.base + p.k * self.half, self.half), :]
        if p.K > 1:
            self.core.wait_recv()
            value = value + self.core_in[pl.ds(self.half_at, self.half), :]
        self.kept[pl.ds(self.half_at, self.half), :] = value
        count = len(p.square)
        for g in range(count):
            self.out[g, self.small, :] = value[g * self.piece : (g + 1) * self.piece].astype(BF16)
        if count > 1:
            some = self.inn.at[pl.ds(0, count - 1), self.small]
            self.square = self.group(1, some, some, p.square_peers[0][1])
            for other, where in p.square_peers:
                self.square.push(
                    self.out.at[other, self.small], self.inn.at[p.g, self.small], where
                )

    def square_take(self):
        p = self.p
        value = self.kept[rows_at(self.half_at + p.g * self.piece, self.piece), :]
        if len(p.square) > 1:
            self.square.wait_recv()
            for other, _ in p.square_peers:
                value = value + self.inn[other, self.small, :].astype(F32)
        self.z_in[p.z, self.small, :] = value.astype(BF16)
        if p.Z > 1:
            some = self.z_in.at[pl.ds(0, p.Z - 1), self.small]
            self.line = self.group(2, some, some, p.z_peers[0][1])
            spot = self.z_in.at[p.z, self.small]
            for _, where in p.z_peers:
                self.line.push(spot, spot, where)

    def line_take(self, factor):
        p = self.p
        if p.Z > 1:
            self.line.wait_recv()
        value = self.z_in[0, self.small, :].astype(F32)
        for i in range(1, p.Z):
            value = value + self.z_in[i, self.small, :].astype(F32)
        spot = rows_at(self.mine, self.piece)
        self.result[spot, :] = (value * factor).astype(BF16)
        count = len(p.square)
        if count > 1:
            some = self.result.at[pl.ds(self.base, (count - 1) * self.piece)]
            self.spread = self.group(3, some, some, p.square_peers[0][1])
            for _, where in p.square_peers:
                self.spread.push(self.result.at[spot], self.result.at[spot], where)

    def spread_take(self):
        p = self.p
        if len(p.square) > 1:
            self.spread.wait_recv()
        if p.K > 1:
            spot = self.result.at[rows_at(self.base + p.k * self.half, self.half)]
            self.last = self.group(4, spot, spot, p.partner)
            self.last.push(spot, spot, p.partner)

    def finish(self):
        if self.p.K > 1:
            self.last.wait_recv()


class Place:
    def __init__(self, n_dom, n_batch):
        self.D = n_dom
        self.Z, self.Y = halves(n_dom)
        self.X, self.K = halves(n_batch)
        self.me = lax.axis_index("dom")
        batch = lax.axis_index("batch")
        self.z, self.y = lax.div(self.me, self.Y), lax.rem(self.me, self.Y)
        self.x, self.k = lax.div(batch, self.K), lax.rem(batch, self.K)
        self.other_k = lax.rem(self.k + 1, self.K)
        self.partner = {"batch": self.x * self.K + self.other_k}
        self.dom_peers = [lax.rem(self.me + d, n_dom) for d in range(1, n_dom)]
        self.z_peers = []
        for d in range(1, self.Z):
            seat = lax.rem(self.z + d, self.Z)
            self.z_peers.append((seat, {"dom": seat * self.Y + self.y}))
        self.y_peers = []
        for d in range(1, self.Y):
            seat = lax.rem(self.y + d, self.Y)
            self.y_peers.append((seat, {"dom": self.z * self.Y + seat}))
        assert self.Z & (self.Z - 1) == 0
        self.seat = flipped(self.z, self.Z)
        self.depth = self.Z.bit_length() - 1
        self.z_pairs = []
        for i in range(self.depth):
            stride = self.Z >> (i + 1)
            other = self.z + stride - 2 * stride * lax.rem(lax.div(self.z, stride), 2)
            kept = self.seat - lax.rem(self.seat, 1 << i)
            given = kept + (1 << i) - 2 * (1 << i) * lax.rem(lax.div(kept, 1 << i), 2)
            self.z_pairs.append((kept, given, {"dom": other * self.Y + self.y}))
        self.square = range(self.X * self.Y)
        self.g = self.x * self.Y + self.y
        self.square_peers = []
        for d in range(1, self.X * self.Y):
            seat = lax.rem(self.g + d, self.X * self.Y)
            where = {
                "batch": lax.div(seat, self.Y) * self.K + self.k,
                "dom": self.z * self.Y + lax.rem(seat, self.Y),
            }
            self.square_peers.append((seat, where))

    def greet(self):
        barrier = pltpu.get_barrier_semaphore()
        peers = [{"dom": other} for other in self.dom_peers]
        if self.K > 1:
            peers.append(self.partner)
        for x in range(1, self.X):
            for y in range(self.Y):
                peers.append(
                    {
                        "batch": lax.rem(self.x + x, self.X) * self.K + self.k,
                        "dom": self.z * self.Y + lax.rem(self.y + y, self.Y),
                    }
                )
        for where in peers:
            pl.semaphore_signal(barrier, inc=1, device_id=where, device_id_type=MESH)
        return lambda: pl.semaphore_wait(barrier, len(peers))


def main_kernel(
    n_dom,
    n_batch,
    hub_w,
    factor,
    sig_ref,
    cot_ref,
    conv_ref,
    mix_ref,
    own_ref,
    own_t_ref,
    far_ref,
    far_t_ref,
    gather_ref,
    scatter_ref,
    layer_ref,
    sgrad_ref,
    result_ref,
    wide_ref,
    wide_t_ref,
    cot_t_ref,
    taps_ref,
    hidden_ref,
    hop_ref,
    back_ref,
    back_one_ref,
    slope_filt,
    slope_gate,
    hop_sum,
    back_sum,
    held_ref,
    sgrad_wide,
    grads_ref,
    out_b,
    hub_b,
    hub_in,
    hub_sum,
    hub_land,
    hub_out,
    in_b,
    out_f,
    in_f,
    core_in,
    kept,
    square_out,
    square_in,
    z_in,
    halo_send,
    halo_recv,
    hub_send,
    hub_recv,
    seg_send,
    seg_recv,
):
    steps, nodes, chans = cot_ref.shape
    p = Place(n_dom, n_batch)
    D, Z, Y = p.D, p.Z, p.Y
    ready = p.greet()
    halo = gather_ref.shape[0] - hub_w
    hw = halo // D
    trail = []
    span = [slice(t * chans, (t + 1) * chans) for t in range(steps + 1)]
    pair = [slice(t * chans, (t + 2) * chans) for t in range(steps)]

    def group(sems, e, kind, t, sent, landed, where):
        return Group(
            trail, sems[0].at[e, kind, t], sems[1].at[e, kind, t], sent, landed, where
        )

    halo_sems, hub_sems = (halo_send, halo_recv), (hub_send, hub_recv)
    groups = {}

    def send_halo(e, kind, t):
        out, inn = (out_b, in_b) if kind == 0 else (out_f, in_f)
        some = inn.at[e, t, pl.ds(0, (D - 1) * hw)]
        g = group(halo_sems, e, kind, t, some, some, {"dom": p.dom_peers[0]})
        mine = rows_at(p.me * hw, hw)
        for other in p.dom_peers:
            g.push(
                out.at[e, t, rows_at(other * hw, hw)], inn.at[e, t, mine], {"dom": other}
            )
        groups["halo", e, kind, t] = g
        inn[e, t, mine, :] = out[e, t, mine, :]

    def send_hub_b(e, t):
        if Y == 1:
            return
        g = group(hub_sems, e, 0, t, hub_in.at[e, t], hub_in.at[e, t], p.y_peers[0][1])
        for seat, where in p.y_peers:
            g.push(
                out_b.at[e, t, rows_at(halo + seat * (Z * hub_w), Z * hub_w)],
                hub_in.at[e, t],
                where,
            )
        groups["hub", e, 0, t] = g

    def pair_b(e, t, i):
        kept, given, where = p.z_pairs[i]
        count = hub_w << i
        spot = rows_at(given * hub_w, count)
        hub_out[e, t, spot, :] = hub_sum[e, t, spot, :].astype(BF16)
        if i == 0:
            land = in_b.at[e, t, pl.ds(halo + hub_w, hub_w)]
        else:
            land = hub_land.at[e, t, pl.ds(count, count)]
        g = group(hub_sems, e, 1 + i, t, land, land, where)
        g.push(hub_out.at[e, t, spot], land, where)
        groups["hub", e, 1 + i, t] = g

    def turn_b(e, t, j):
        if j == 0:
            value = hub_b[t, rows_at(p.y * (Z * hub_w), Z * hub_w), :]
            if Y > 1:
                groups["hub", e, 0, t].wait_recv()
                value = value + hub_in[e, t].astype(F32)
            hub_sum[e, t] = value
        else:
            i = p.depth - j
            kept, count = p.z_pairs[i][0], hub_w << i
            groups["hub", e, 1 + i, t].wait_recv()
            hub_sum[e, t, rows_at(kept * hub_w, count), :] += hub_land[
                e, t, pl.ds(count, count), :
            ].astype(F32)
        if j < p.depth:
            pair_b(e, t, p.depth - 1 - j)
        if j == max(p.depth - 1, 0):
            in_b[e, t, pl.ds(halo, hub_w), :] = hub_sum[
                e, t, rows_at(p.seat * hub_w, hub_w), :
            ].astype(BF16)

    def take_b(e, t):
        if D > 1:
            groups["halo", e, 0, t].wait_recv()
        if Z > 1:
            groups["hub", e, 1, t].wait_recv()
        return nn(scatter_ref[...], in_b[e, t])

    def pair_f(e, t, i):
        kept, given, where = p.z_pairs[i]
        base, count = halo + p.y * (Z * hub_w), hub_w << i
        land = in_f.at[e, t, rows_at(base + given * hub_w, count)]
        spot = in_f.at[e, t, rows_at(base + kept * hub_w, count)]
        source = out_f.at[e, t, pl.ds(halo, hub_w)] if i == 0 else spot
        g = group(hub_sems, e, 1 + p.depth + i, t, land, land, where)
        g.push(source, spot, where)
        groups["row", e, i, t] = g

    def column_f(e, t):
        if Y == 1:
            return
        column = in_f.at[e, t, rows_at(halo + p.y * (Z * hub_w), Z * hub_w)]
        g = group(hub_sems, e, 1 + 2 * p.depth, t, column, column, p.y_peers[0][1])
        for _, where in p.y_peers:
            g.push(column, column, where)
        groups["row", e, p.depth, t] = g

    def send_hub_f(e, t):
        mine = rows_at(halo + (p.y * Z + p.seat) * hub_w, hub_w)
        in_f[e, t, mine, :] = out_f[e, t, halo:, :]
        if p.depth:
            pair_f(e, t, 0)
        else:
            column_f(e, t)

    def turn_f(e, t, j):
        if j >= p.depth:
            return
        groups["row", e, j, t].wait_recv()
        if j + 1 < p.depth:
            pair_f(e, t, j + 1)
        else:
            column_f(e, t)

    def take_f(e, t):
        if D > 1:
            groups["halo", e, 1, t].wait_recv()
        if Y > 1:
            groups["row", e, p.depth, t].wait_recv()
        return nn(far_ref[...], in_f[e, t])

    def first(turn, e):
        for t in range(steps):
            turn(e, t, 0)

    def rest(turn, e):
        for j in range(1, max(p.depth, 1)):
            for t in range(steps):
                turn(e, t, j)

    def put_b(e, t, field):
        value = nn(far_t_ref[...], field)
        out_b[e, t] = value.astype(BF16)
        hub_b[t] = value[halo:]

    def segment(number, base, rows):
        refs = (
            grads_ref,
            core_in,
            kept,
            square_out,
            square_in,
            z_in,
            result_ref,
            seg_send,
            seg_recv,
        )
        return Segment(p, number, base * chans, rows * chans, refs, trail)

    filt_seg, gate_seg, mix_seg, last_seg = (
        segment(0, 0, 2),
        segment(1, 2, 2),
        segment(2, 4, 2),
        segment(3, 6, 1),
    )

    for t in range(steps):
        back = nt(cot_ref[t], mix_ref[2]).astype(BF16)
        back_ref[t] = back
        put_b(0, t, back)
        if t == 0:
            ready()
        send_hub_b(0, t)
        send_halo(0, 0, t)

    wide_ref[...] = sig_ref[...].reshape(nodes, (steps + 1) * chans)
    for kind in range(2):
        for tap in range(2):
            taps_ref[span[tap], span[kind]] = conv_ref[kind, tap]
    edge = nn(gather_ref[...], wide_ref[...]).astype(BF16)
    for t in range(steps):
        both = nn(edge[:, pair[t]], taps_ref[...])
        out_f[0, t] = (jnp.tanh(both[:, :chans]) * jax.nn.sigmoid(both[:, chans:])).astype(BF16)
        send_hub_f(0, t)

    def convolve(t):
        both = nn(wide_ref[:, pair[t]], taps_ref[...])
        tanh_filt = jnp.tanh(both[:, :chans])
        sig_gate = jax.nn.sigmoid(both[:, chans:])
        hidden_ref[t] = (tanh_filt * sig_gate).astype(BF16)
        slope_filt[t] = sig_gate * (1.0 - tanh_filt * tanh_filt)
        slope_gate[t] = tanh_filt * sig_gate * (1.0 - sig_gate)

    for t in range(steps):
        back_sum[t] = nt(cot_ref[t], mix_ref[1]) + nn(own_t_ref[...], back_ref[t])
    first(turn_b, 0)
    send_halo(0, 1, 0)
    for t in range(steps - 1):
        convolve(t)
    first(turn_f, 0)
    rest(turn_b, 0)
    for t in range(1, steps):
        send_halo(0, 1, t)
    convolve(steps - 1)
    rest(turn_f, 0)

    for t in range(steps):
        back = (back_sum[t] + take_b(0, t)).astype(BF16)
        back_one_ref[t] = back
        put_b(1, t, back)
        send_hub_b(1, t)
        send_halo(1, 0, t)
    for t in range(steps):
        hop_sum[t] = nn(own_ref[...], hidden_ref[t])
    for t in range(steps):
        back_sum[t] = nt(cot_ref[t], mix_ref[0]) + nn(own_t_ref[...], back_one_ref[t])
    wide_t_ref[...] = wide_ref[...].T
    first(turn_b, 1)

    for t in range(steps):
        hop = (hop_sum[t] + take_f(0, t)).astype(BF16)
        hop_ref[t] = hop
        out_f[1, t] = nn(gather_ref[...], hop).astype(BF16)
        send_hub_f(1, t)
        if t == 0:
            send_halo(1, 1, t)
    rest(turn_b, 1)
    for t in range(1, steps):
        send_halo(1, 1, t)

    for t in range(steps):
        cot_t_ref[t] = cot_ref[t].T
    for spot, field in enumerate((hidden_ref, hop_ref)):
        part = nn(cot_t_ref[0], field[0])
        for t in range(1, steps):
            part += nn(cot_t_ref[t], field[t])
        grads_ref[(4 + spot) * chans : (5 + spot) * chans, :] = part.T
    mix_seg.core_send()
    first(turn_f, 1)

    for t in range(steps):
        grad_hidden = back_sum[t] + take_b(1, t)
        held_ref[t, :, :chans] = (grad_hidden * slope_filt[t]).astype(BF16)
        held_ref[t, :, chans:] = (grad_hidden * slope_gate[t]).astype(BF16)
    for kind, seg in enumerate((filt_seg, gate_seg)):
        outer = nn(wide_t_ref[pair[0], :], held_ref[0, :, span[kind]])
        for t in range(1, steps):
            outer += nn(wide_t_ref[pair[t], :], held_ref[t, :, span[kind]])
        grads_ref[kind * 2 * chans : (kind + 1) * 2 * chans, :] = outer
        seg.core_send()
    rest(turn_f, 1)
    mix_seg.core_take()
    for t in range(steps):
        hop_sum[t] = nn(own_ref[...], hop_ref[t])
    filt_seg.core_take()
    gate_seg.core_take()
    mix_seg.square_take()

    part = None
    for t in range(steps):
        hop = (hop_sum[t] + take_f(1, t)).astype(BF16)
        hop_sum[t] = nn(hop, mix_ref[2])
        here = nn(cot_t_ref[t], hop)
        part = here if part is None else part + here
    grads_ref[6 * chans :, :] = part.T
    last_seg.core_send()
    filt_seg.square_take()
    gate_seg.square_take()
    last_seg.core_take()
    for t in range(steps):
        layer_ref[t] = (
            wide_ref[:, span[t + 1]].astype(F32)
            + nn(hidden_ref[t], mix_ref[0])
            + nn(hop_ref[t], mix_ref[1])
            + hop_sum[t]
        ).astype(BF16)
    last_seg.square_take()
    carried = None
    for t in range(steps):
        into = nt(held_ref[t], taps_ref[...])
        before = into[:, :chans]
        if t > 0:
            before = before + carried
        sgrad_wide[:, span[t]] = before.astype(BF16)
        carried = into[:, chans:] + cot_ref[t].astype(F32)
    sgrad_wide[:, span[steps]] = carried.astype(BF16)
    sgrad_ref[...] = sgrad_wide[...].reshape(sgrad_ref.shape)
    order = (mix_seg, filt_seg, gate_seg, last_seg)
    for seg in order:
        seg.line_take(factor)
    for seg in order:
        seg.spread_take()
    for seg in order:
        seg.finish()
    for g in trail:
        g.wait_send()


def finish_kernel(layer_ref, sgrad_ref, result_ref, layer_out, sgrad_out, conv_out, mix_out, sems):
    copies = [
        pltpu.make_async_copy(layer_ref, layer_out, sems.at[0]),
        pltpu.make_async_copy(sgrad_ref, sgrad_out, sems.at[1]),
    ]
    for copy in copies:
        copy.start()
    rows = conv_out.shape[0]
    conv_out[...] = result_ref[:rows, :].astype(F32)
    mix_out[...] = result_ref[rows:, :].astype(F32)
    for copy in copies:
        copy.wait()


def shape_of(*dims, dtype=BF16):
    return jax.ShapeDtypeStruct(dims, dtype)


def room_for(scratch):
    sizes = (
        math.prod(part.shape) * jnp.dtype(part.dtype).itemsize
        for part in scratch
        if part.memory_space == pltpu.VMEM
    )
    return min(sum(sizes) + (10 << 20), 60 * 1024 * 1024)


def body(
    axis_sizes,
    signal,
    cotangent,
    conv_weight,
    mix_weight,
    send_rows,
    send_mask,
    tile_vals,
    tile_row,
    tile_col,
    tile_mask,
    hub_owner,
    hub_rows,
):
    nodes, b_dev, hist, chans = signal.shape
    steps = hist - 1
    n_dom, cap = send_rows.shape
    n_batch = dict(axis_sizes)["batch"]
    outer, inner = halves(n_dom)
    square = halves(n_batch)[0] * inner
    pair = halves(n_batch)[1]
    hub_per = hub_rows.shape[1]
    hw, hub_w = padded(cap), padded(hub_per)
    halo = n_dom * hw
    slots = halo + n_dom * hub_w
    back_rows = halo + min(outer, 2) * hub_w
    lead_rows = halo + hub_w
    block = tile_vals.shape[1]
    entries = n_dom * cap + hub_rows.size
    all_tiles = (nodes + entries) // block

    sig = signal.reshape(nodes, hist, chans)
    cot = jnp.transpose(cotangent.reshape(nodes, steps, chans), (1, 0, 2))

    parts = [part[None] for part in (tile_row, tile_col, tile_mask, hub_owner)]
    parts += [send_rows, send_mask, hub_rows]
    most = max(part.shape[1] for part in parts)
    table = jnp.concatenate(
        [jnp.pad(part, ((0, 0), (0, most - part.shape[1]))) for part in parts]
    )
    mats = pl.pallas_call(
        functools.partial(build_kernel, outer, inner, n_dom, hub_w, cap, hub_per),
        out_shape=(
            shape_of(nodes, nodes),
            shape_of(nodes, nodes),
            shape_of(nodes, slots),
            shape_of(slots, nodes),
            shape_of(lead_rows, nodes),
            shape_of(nodes, back_rows),
        ),
        in_specs=[HBM] * 2,
        out_specs=(VMEM,) * 6,
        scratch_shapes=[
            pltpu.VMEM((all_tiles, nodes, block), F32),
            pltpu.VMEM((entries, slots), BF16),
            pltpu.SMEM(table.shape, jnp.int32),
            pltpu.VMEM(table.shape, jnp.int32),
            pltpu.VMEM(tile_vals.shape, BF16),
            pltpu.SemaphoreType.DMA((3,)),
        ],
        compiler_params=pltpu.CompilerParams(vmem_limit_bytes=BUILD_ROOM),
        cost_estimate=pl.CostEstimate(flops=3 * 10**9, bytes_accessed=10**7, transcendentals=0),
        name="build",
    )(
        table,
        tile_vals,
    )

    total_count = nodes * steps * b_dev
    for _, size in axis_sizes:
        total_count *= size
    weights = 7 * chans
    field = pltpu.VMEM((steps, nodes, chans), BF16)
    total = pltpu.VMEM((steps, nodes, chans), F32)
    wide = pltpu.VMEM((nodes, hist * chans), BF16)
    halo_sems = pltpu.SemaphoreType.DMA((2, 2, steps))
    hub_sems = pltpu.SemaphoreType.DMA((2, 2 * outer.bit_length(), steps))
    seg_sems = pltpu.SemaphoreType.DMA((4, 5))
    scratch = [
        wide,
        pltpu.VMEM((hist * chans, nodes), BF16),
        pltpu.VMEM((steps, chans, nodes), BF16),
        pltpu.VMEM((2 * chans, 2 * chans), BF16),
        field,
        field,
        field,
        field,
        total,
        total,
        total,
        total,
        pltpu.VMEM((steps, nodes, 2 * chans), BF16),
        wide,
        pltpu.VMEM((weights, chans), F32),
        pltpu.VMEM((2, steps, slots, chans), BF16),
        pltpu.VMEM((steps, n_dom * hub_w, chans), F32),
        pltpu.VMEM((2, steps, outer * hub_w, chans), BF16),
        pltpu.VMEM((2, steps, outer * hub_w, chans), F32),
        pltpu.VMEM((2, steps, outer * hub_w, chans), BF16),
        pltpu.VMEM((2, steps, outer * hub_w, chans), BF16),
        pltpu.VMEM((2, steps, back_rows, chans), BF16),
        pltpu.VMEM((2, steps, lead_rows, chans), BF16),
        pltpu.VMEM((2, steps, slots, chans), BF16),
        pltpu.VMEM((weights // pair, chans), F32),
        pltpu.VMEM((weights // pair, chans), F32),
        pltpu.VMEM((square, weights // (pair * square), chans), BF16),
        pltpu.VMEM((square, weights // (pair * square), chans), BF16),
        pltpu.VMEM((outer, weights // (pair * square), chans), BF16),
        halo_sems,
        halo_sems,
        hub_sems,
        hub_sems,
        seg_sems,
        seg_sems,
    ]
    layer, sgrad, result = pl.pallas_call(
        functools.partial(
            main_kernel, n_dom, n_batch, hub_w, 1.0 / math.sqrt(total_count)
        ),
        out_shape=(
            shape_of(steps, nodes, chans),
            shape_of(nodes, hist, chans),
            shape_of(weights, chans),
        ),
        in_specs=[VMEM] * 10,
        out_specs=(VMEM,) * 3,
        scratch_shapes=scratch,
        compiler_params=pltpu.CompilerParams(
            collective_id=0, has_side_effects=True, vmem_limit_bytes=room_for(scratch)
        ),
        name="main",
    )(sig, cot, conv_weight, mix_weight, *mats)

    layer_out, signal_grad, conv_grad, mix_grad = pl.pallas_call(
        finish_kernel,
        out_shape=(
            shape_of(steps, nodes, chans),
            shape_of(nodes, hist, chans),
            shape_of(4 * chans, chans, dtype=F32),
            shape_of(3 * chans, chans, dtype=F32),
        ),
        in_specs=[VMEM] * 3,
        out_specs=(ANY, ANY, VMEM, VMEM),
        scratch_shapes=[pltpu.SemaphoreType.DMA((2,))],
        compiler_params=pltpu.CompilerParams(vmem_limit_bytes=12 << 20),
        name="finish",
    )(layer, sgrad, result)
    return (
        jnp.transpose(layer_out, (1, 0, 2)).reshape(nodes, b_dev, steps, chans),
        signal_grad.reshape(signal.shape),
        conv_grad.reshape(conv_weight.shape),
        mix_grad.reshape(mix_weight.shape),
    )


def solution(mesh):
    placed = (
        P("dom", "batch", None, None),
        P("dom", "batch", None, None),
        P(),
        P(),
        P("dom", None),
        P("dom", None),
        P("dom", None, None),
        P("dom"),
        P("dom"),
        P("dom"),
        P(),
        P(),
    )
    axis_sizes = tuple((axis, mesh.shape[axis]) for axis in ("dom", "batch"))
    return jax.shard_map(
        functools.partial(body, axis_sizes),
        mesh=mesh,
        in_specs=placed,
        out_specs=(P("dom", "batch", None, None), P("dom", "batch", None, None), P(), P()),
        check_vma=False,
    )
```

```python
import functools
import math

import jax
import jax.numpy as jnp
from jax import lax
from jax.experimental import pallas as pl
from jax.experimental.pallas import tpu as pltpu
from jax.sharding import PartitionSpec as P

VMEM = pl.BlockSpec(memory_space=pltpu.VMEM)
ANY = pl.BlockSpec(memory_space=pl.ANY)
HBM = pl.BlockSpec(memory_space=pltpu.HBM)
MESH = pl.DeviceIdType.MESH
BUILD_ROOM = 52 << 20
F32 = jnp.float32
BF16 = jnp.bfloat16


def nn(left, right):
    return lax.dot_general(left, right, (((1,), (0,)), ((), ())), preferred_element_type=F32)


def nt(left, right):
    return lax.dot_general(left, right, (((1,), (1,)), ((), ())), preferred_element_type=F32)


def halves(size):
    return (size // 2, 2) if size % 2 == 0 else (size, 1)


def flipped(index, size):
    total, low, high = 0, 1, size // 2
    while high >= 1:
        total = total + lax.rem(lax.div(index, low), 2) * high
        low, high = low * 2, high // 2
    return total


def padded(rows):
    return -(-rows // 16) * 16


def build_kernel(
    outer,
    inner,
    n_dom,
    hub_width,
    cap,
    hub_per,
    table_any,
    tile_any,
    own_ref,
    own_t_ref,
    far_ref,
    far_t_ref,
    gather_ref,
    scatter_ref,
    dense_ref,
    place_ref,
    ints_ref,
    table_ref,
    tile_ref,
    sems,
):
    loads = [
        pltpu.make_async_copy(source, target, sems.at[i])
        for i, (source, target) in enumerate(
            (
                (table_any, ints_ref),
                (table_any, table_ref),
                (tile_any, tile_ref),
            )
        )
    ]
    for load in loads:
        load.start()
    nodes = own_ref.shape[0]
    tiles, block, _ = tile_ref.shape
    own_tiles = nodes // block
    all_tiles = dense_ref.shape[0]
    slots = far_ref.shape[1]
    groups = ints_ref.shape[0] - 4 - 2 * n_dom
    rows_ref, flag_ref = table_ref.at[4 : 4 + n_dom], table_ref.at[4 + n_dom : 4 + 2 * n_dom]
    hubs_ref = table_ref.at[4 + 2 * n_dom :]
    halo_slots = gather_ref.shape[0] - hub_width
    halo_width = halo_slots // n_dom
    halo = n_dom * cap

    dense_ref[...] = jnp.zeros_like(dense_ref)
    entry = lax.broadcasted_iota(jnp.int32, (halo, slots), 0)
    if cap != halo_width:
        entry = lax.div(entry, cap) * halo_width + lax.rem(entry, cap)
    place_ref[:halo, :] = jnp.where(
        entry == lax.broadcasted_iota(jnp.int32, (halo, slots), 1), 1.0, 0.0
    ).astype(BF16)
    source = lax.div(lax.broadcasted_iota(jnp.int32, (halo_slots, n_dom), 0), halo_width)
    expand = (source == lax.broadcasted_iota(jnp.int32, (halo_slots, n_dom), 1)).astype(F32)
    lane = lax.rem(lax.broadcasted_iota(jnp.int32, (halo_slots, cap), 0), halo_width)
    for load in loads:
        load.wait()
    for t in range(tiles):

        @pl.when(ints_ref[2, t] == 1)
        def _():
            rows = pl.ds(pl.multiple_of(ints_ref[0, t] * block, block), block)
            dense_ref[ints_ref[1, t], rows, :] += tile_ref[t].astype(F32)

    slot = lax.broadcasted_iota(jnp.int32, (hub_per, slots), 1)
    entry = lax.broadcasted_iota(jnp.int32, (hub_per, slots), 0) + halo_slots
    me = lax.axis_index("dom")
    hub = jnp.zeros((1, hub_per), F32)
    for o in range(groups):
        at = halo + o * hub_per
        owner = ints_ref[3, o]
        seat = lax.rem(owner, inner) * outer + flipped(lax.div(owner, inner), outer)
        place_ref[at : at + hub_per, :] = jnp.where(
            slot == entry + seat * hub_width, 1.0, 0.0
        ).astype(BF16)
        owned = (owner == me).astype(F32)
        hub += owned * (hubs_ref[o : o + 1, :hub_per].astype(F32) + 1.0)
    far = nn(dense_ref[own_tiles].astype(BF16), place_ref[:block, :])
    for c in range(own_tiles + 1, all_tiles):
        at = (c - own_tiles) * block
        far += nn(dense_ref[c].astype(BF16), place_ref[at : at + block, :])
    far_ref[...] = far.astype(BF16)
    far_t_ref[...] = far.T.astype(BF16)
    for c in range(own_tiles):
        part = dense_ref[c]
        own_ref[:, c * block : (c + 1) * block] = part.astype(BF16)
        own_t_ref[c * block : (c + 1) * block, :] = part.T.astype(BF16)

    chosen = jnp.where(flag_ref[:, :cap] == 1, rows_ref[:, :cap].astype(F32) + 1.0, 0.0)
    spread = jnp.dot(
        expand, chosen, precision=lax.Precision.HIGHEST, preferred_element_type=F32
    )
    from_halo = jnp.where(
        lax.broadcasted_iota(jnp.int32, (halo_slots, cap), 1) == lane, spread, 0.0
    )
    from_hub = jnp.where(
        lax.broadcasted_iota(jnp.int32, (hub_width, hub_per), 1)
        == lax.broadcasted_iota(jnp.int32, (hub_width, hub_per), 0),
        jnp.broadcast_to(hub, (hub_width, hub_per)),
        0.0,
    )

    def picked(values):
        pick = (jnp.sum(values, axis=1, keepdims=True) + 0.5).astype(jnp.int32) - 1
        node = lax.broadcasted_iota(jnp.int32, (values.shape[0], nodes), 1)
        return jnp.where(pick == node, 1.0, 0.0)

    halo_pick, hub_pick = picked(from_halo), picked(from_hub)
    gather_ref[:halo_slots, :] = halo_pick.astype(BF16)
    gather_ref[halo_slots:, :] = hub_pick.astype(BF16)
    scatter_ref[...] = (
        jnp.concatenate([halo_pick] + [hub_pick] * outer, axis=0).T.astype(BF16)
    )


def rows_at(start, count):
    return pl.ds(pl.multiple_of(start, 16), count)


class Group:
    def __init__(self, trail, send_sem, recv_sem, sent, landed, where):
        self.send_sem, self.recv_sem = send_sem, recv_sem
        self.sent, self.landed, self.where = sent, landed, where
        trail.append(self)

    def push(self, source, target, where):
        pltpu.make_async_remote_copy(
            src_ref=source,
            dst_ref=target,
            send_sem=self.send_sem,
            recv_sem=self.recv_sem,
            device_id=where,
            device_id_type=MESH,
        ).start()

    def whole(self):
        return pltpu.make_async_remote_copy(
            src_ref=self.sent,
            dst_ref=self.landed,
            send_sem=self.send_sem,
            recv_sem=self.recv_sem,
            device_id=self.where,
            device_id_type=MESH,
        )

    def wait_recv(self):
        self.whole().wait_recv()

    def wait_send(self):
        self.whole().wait_send()


class Segment:
    def __init__(self, place, number, base, rows, refs, trail):
        self.p, self.n, self.base, self.rows, self.trail = place, number, base, rows, trail
        (self.grads, self.core_in, self.kept, self.out, self.inn, self.z_in, self.result) = refs[:7]
        self.send_sem, self.recv_sem = refs[7:]
        p = place
        self.half = rows // p.K
        self.piece = self.half // len(p.square)
        self.half_at = base // p.K
        self.piece_at = base // (p.K * len(p.square))
        self.mine = base + p.k * self.half + p.g * self.piece
        self.small = pl.ds(self.piece_at, self.piece)

    def group(self, stage, sent, landed, where):
        return Group(
            self.trail,
            self.send_sem.at[self.n, stage],
            self.recv_sem.at[self.n, stage],
            sent,
            landed,
            where,
        )

    def core_send(self):
        p = self.p
        if p.K == 1:
            return
        spot = self.core_in.at[pl.ds(self.half_at, self.half)]
        self.core = self.group(0, spot, spot, p.partner)
        give = self.base + p.other_k * self.half
        self.core.push(self.grads.at[rows_at(give, self.half)], spot, p.partner)

    def core_take(self):
        p = self.p
        value = self.grads[rows_at(self.base + p.k * self.half, self.half), :]
        if p.K > 1:
            self.core.wait_recv()
            value = value + self.core_in[pl.ds(self.half_at, self.half), :]
        self.kept[pl.ds(self.half_at, self.half), :] = value
        count = len(p.square)
        for g in range(count):
            self.out[g, self.small, :] = value[g * self.piece : (g + 1) * self.piece].astype(BF16)
        if count > 1:
            some = self.inn.at[pl.ds(0, count - 1), self.small]
            self.square = self.group(1, some, some, p.square_peers[0][1])
            for other, where in p.square_peers:
                self.square.push(
                    self.out.at[other, self.small], self.inn.at[p.g, self.small], where
                )

    def square_take(self):
        p = self.p
        value = self.kept[rows_at(self.half_at + p.g * self.piece, self.piece), :]
        if len(p.square) > 1:
            self.square.wait_recv()
            for other, _ in p.square_peers:
                value = value + self.inn[other, self.small, :].astype(F32)
        self.z_in[p.z, self.small, :] = value.astype(BF16)
        if p.Z > 1:
            some = self.z_in.at[pl.ds(0, p.Z - 1), self.small]
            self.line = self.group(2, some, some, p.z_peers[0][1])
            spot = self.z_in.at[p.z, self.small]
            for _, where in p.z_peers:
                self.line.push(spot, spot, where)

    def line_take(self, factor):
        p = self.p
        if p.Z > 1:
            self.line.wait_recv()
        value = self.z_in[0, self.small, :].astype(F32)
        for i in range(1, p.Z):
            value = value + self.z_in[i, self.small, :].astype(F32)
        spot = rows_at(self.mine, self.piece)
        self.result[spot, :] = (value * factor).astype(BF16)
        count = len(p.square)
        if count > 1:
            some = self.result.at[pl.ds(self.base, (count - 1) * self.piece)]
            self.spread = self.group(3, some, some, p.square_peers[0][1])
            for _, where in p.square_peers:
                self.spread.push(self.result.at[spot], self.result.at[spot], where)

    def spread_take(self):
        p = self.p
        if len(p.square) > 1:
            self.spread.wait_recv()
        if p.K > 1:
            spot = self.result.at[rows_at(self.base + p.k * self.half, self.half)]
            self.last = self.group(4, spot, spot, p.partner)
            self.last.push(spot, spot, p.partner)

    def finish(self):
        if self.p.K > 1:
            self.last.wait_recv()


class Direct:
    def __init__(self, place, number, base, rows, refs, trail):
        self.p, self.base, self.rows, self.trail = place, base, rows, trail
        self.grads, self.core_in, self.kept, self.out, self.inn, self.result = refs[:6]
        self.send_sem, self.recv_sem = refs[6].at[number], refs[7].at[number]
        self.lanes = self.grads.shape[1] // place.K
        self.piece = rows // len(place.chips)
        self.half = pl.ds(pl.multiple_of(place.k * self.lanes, 128), self.lanes)
        self.mine = rows_at(base + place.c * self.piece, self.piece)

    def group(self, stage, sent, landed, where):
        return Group(
            self.trail, self.send_sem.at[stage], self.recv_sem.at[stage], sent, landed, where
        )

    def core_send(self):
        p = self.p
        if p.K == 1:
            return
        other = pl.ds(pl.multiple_of(p.other_k * self.lanes, 128), self.lanes)
        self.core = self.group(0, self.core_in, self.core_in, p.partner)
        self.core.push(
            self.grads.at[pl.ds(self.base, self.rows), other], self.core_in, p.partner
        )

    def core_take(self):
        p = self.p
        value = self.grads[pl.ds(self.base, self.rows), self.half]
        if p.K > 1:
            self.core.wait_recv()
            value = value + self.core_in[...]
        self.kept[...] = value
        self.out[...] = value.astype(BF16)
        count = len(p.chips)
        if count > 1:
            some = self.inn.at[pl.ds(0, (count - 1) * self.piece)]
            self.chip = self.group(1, some, some, p.chip_peers[0][1])
            for other, where in p.chip_peers:
                self.chip.push(
                    self.out.at[rows_at(other * self.piece, self.piece)],
                    self.inn.at[rows_at(p.c * self.piece, self.piece)],
                    where,
                )

    def chip_take(self, factor):
        p = self.p
        value = self.kept[rows_at(p.c * self.piece, self.piece), :]
        if len(p.chips) > 1:
            self.chip.wait_recv()
            for other, _ in p.chip_peers:
                value = value + self.inn[rows_at(other * self.piece, self.piece), :].astype(F32)
        self.result[self.mine, self.half] = (value * factor).astype(BF16)
        if len(p.chips) > 1:
            rows = pl.ds(self.base, (len(p.chips) - 1) * self.piece)
            some = self.result.at[rows, self.half]
            self.spread = self.group(3, some, some, p.chip_peers[0][1])
            spot = self.result.at[self.mine, self.half]
            for _, where in p.chip_peers:
                self.spread.push(spot, spot, where)

    def square_take(self):
        pass

    def line_take(self, factor):
        self.chip_take(factor)

    def spread_take(self):
        p = self.p
        if len(p.chips) > 1:
            self.spread.wait_recv()
        if p.K > 1:
            spot = self.result.at[pl.ds(self.base, self.rows), self.half]
            self.last = self.group(4, spot, spot, p.partner)
            self.last.push(spot, spot, p.partner)

    def finish(self):
        if self.p.K > 1:
            self.last.wait_recv()


def direct_fits(chips, cores, chans):
    return chans % (chips * 16) == 0 and chans % (cores * 128) == 0


class Place:
    def __init__(self, n_dom, n_batch):
        self.D = n_dom
        self.Z, self.Y = halves(n_dom)
        self.X, self.K = halves(n_batch)
        self.me = lax.axis_index("dom")
        batch = lax.axis_index("batch")
        self.z, self.y = lax.div(self.me, self.Y), lax.rem(self.me, self.Y)
        self.x, self.k = lax.div(batch, self.K), lax.rem(batch, self.K)
        self.other_k = lax.rem(self.k + 1, self.K)
        self.partner = {"batch": self.x * self.K + self.other_k}
        self.dom_peers = [lax.rem(self.me + d, n_dom) for d in range(1, n_dom)]
        self.z_peers = []
        for d in range(1, self.Z):
            seat = lax.rem(self.z + d, self.Z)
            self.z_peers.append((seat, {"dom": seat * self.Y + self.y}))
        self.y_peers = []
        for d in range(1, self.Y):
            seat = lax.rem(self.y + d, self.Y)
            self.y_peers.append((seat, {"dom": self.z * self.Y + seat}))
        assert self.Z & (self.Z - 1) == 0
        self.seat = flipped(self.z, self.Z)
        self.depth = self.Z.bit_length() - 1
        self.z_pairs = []
        for i in range(self.depth):
            stride = self.Z >> (i + 1)
            other = self.z + stride - 2 * stride * lax.rem(lax.div(self.z, stride), 2)
            kept = self.seat - lax.rem(self.seat, 1 << i)
            given = kept + (1 << i) - 2 * (1 << i) * lax.rem(lax.div(kept, 1 << i), 2)
            self.z_pairs.append((kept, given, {"dom": other * self.Y + self.y}))
        self.square = range(self.X * self.Y)
        self.g = self.x * self.Y + self.y
        self.square_peers = []
        for d in range(1, self.X * self.Y):
            seat = lax.rem(self.g + d, self.X * self.Y)
            where = {
                "batch": lax.div(seat, self.Y) * self.K + self.k,
                "dom": self.z * self.Y + lax.rem(seat, self.Y),
            }
            self.square_peers.append((seat, where))

        self.chips = range(n_dom * self.X)
        self.c = self.me * self.X + self.x
        self.chip_peers = []
        for d in range(1, n_dom * self.X):
            seat = lax.rem(self.c + d, n_dom * self.X)
            where = {
                "dom": lax.div(seat, self.X),
                "batch": lax.rem(seat, self.X) * self.K + self.k,
            }
            self.chip_peers.append((seat, where))

    def greet(self, everyone):
        barrier = pltpu.get_barrier_semaphore()
        if everyone:
            peers = [where for _, where in self.chip_peers]
        else:
            peers = [{"dom": other} for other in self.dom_peers] + self.across()
        if self.K > 1:
            peers.append(self.partner)
        for where in peers:
            pl.semaphore_signal(barrier, inc=1, device_id=where, device_id_type=MESH)
        return lambda: pl.semaphore_wait(barrier, len(peers))

    def across(self):
        peers = []
        for x in range(1, self.X):
            for y in range(self.Y):
                peers.append(
                    {
                        "batch": lax.rem(self.x + x, self.X) * self.K + self.k,
                        "dom": self.z * self.Y + lax.rem(self.y + y, self.Y),
                    }
                )
        return peers


def main_kernel(
    n_dom,
    n_batch,
    hub_w,
    factor,
    sig_ref,
    cot_ref,
    conv_ref,
    mix_ref,
    own_ref,
    own_t_ref,
    far_ref,
    far_t_ref,
    gather_ref,
    scatter_ref,
    layer_ref,
    sgrad_ref,
    result_ref,
    wide_ref,
    wide_t_ref,
    cot_t_ref,
    taps_ref,
    hidden_ref,
    hop_ref,
    back_ref,
    back_one_ref,
    slope_filt,
    slope_gate,
    hop_sum,
    back_sum,
    layer_sum,
    held_ref,
    sgrad_wide,
    grads_ref,
    out_b,
    hub_b,
    hub_in,
    hub_out,
    in_b,
    out_f,
    in_f,
    core_in,
    kept,
    square_out,
    square_in,
    z_in,
    lane_in,
    lane_kept,
    lane_out,
    lane_land,
    halo_send,
    halo_recv,
    hub_send,
    hub_recv,
    seg_send,
    seg_recv,
):
    steps, nodes, chans = cot_ref.shape
    p = Place(n_dom, n_batch)
    D, Z, Y = p.D, p.Z, p.Y
    chans_fit = direct_fits(len(p.chips), p.K, chans)
    ready = p.greet(chans_fit)
    halo = gather_ref.shape[0] - hub_w
    hw = halo // D
    trail = []
    span = [slice(t * chans, (t + 1) * chans) for t in range(steps + 1)]
    pair = [slice(t * chans, (t + 2) * chans) for t in range(steps)]

    def group(sems, e, kind, t, sent, landed, where):
        return Group(
            trail, sems[0].at[e, kind, t], sems[1].at[e, kind, t], sent, landed, where
        )

    halo_sems, hub_sems = (halo_send, halo_recv), (hub_send, hub_recv)
    groups = {}

    def send_halo(e, kind, t):
        out, inn = (out_b, in_b) if kind == 0 else (out_f, in_f)
        some = inn.at[e, t, pl.ds(0, (D - 1) * hw)]
        g = group(halo_sems, e, kind, t, some, some, {"dom": p.dom_peers[0]})
        mine = rows_at(p.me * hw, hw)
        for other in p.dom_peers:
            g.push(
                out.at[e, t, rows_at(other * hw, hw)], inn.at[e, t, mine], {"dom": other}
            )
        groups["halo", e, kind, t] = g
        inn[e, t, mine, :] = out[e, t, mine, :]

    def send_hub_b(e, t):
        if Y == 1:
            return
        g = group(hub_sems, e, 0, t, hub_in.at[e, t], hub_in.at[e, t], p.y_peers[0][1])
        for seat, where in p.y_peers:
            g.push(
                out_b.at[e, t, rows_at(halo + seat * (Z * hub_w), Z * hub_w)],
                hub_in.at[e, t],
                where,
            )
        groups["hub", e, 0, t] = g

    def turn_b(e, t):
        value = hub_b[t, rows_at(p.y * (Z * hub_w), Z * hub_w), :]
        if Y > 1:
            groups["hub", e, 0, t].wait_recv()
            value = value + hub_in[e, t].astype(F32)
        hub_out[e, t] = value.astype(BF16)
        mine = rows_at(halo + p.z * hub_w, hub_w)
        if Z > 1:
            some = in_b.at[e, t, pl.ds(halo, (Z - 1) * hub_w)]
            g = group(hub_sems, e, 1, t, some, some, p.z_peers[0][1])
            for seat, where in p.z_peers:
                g.push(
                    hub_out.at[e, t, rows_at(flipped(seat, Z) * hub_w, hub_w)],
                    in_b.at[e, t, mine],
                    where,
                )
            groups["hub", e, 1, t] = g
        in_b[e, t, mine, :] = hub_out[e, t, rows_at(p.seat * hub_w, hub_w), :]

    def take_b(e, t):
        if D > 1:
            groups["halo", e, 0, t].wait_recv()
        if Z > 1:
            groups["hub", e, 1, t].wait_recv()
        return nn(scatter_ref[...], in_b[e, t])

    def pair_f(e, t, i):
        kept, given, where = p.z_pairs[i]
        base, count = halo + p.y * (Z * hub_w), hub_w << i
        land = in_f.at[e, t, rows_at(base + given * hub_w, count)]
        spot = in_f.at[e, t, rows_at(base + kept * hub_w, count)]
        source = out_f.at[e, t, pl.ds(halo, hub_w)] if i == 0 else spot
        g = group(hub_sems, e, 2 + i, t, land, land, where)
        g.push(source, spot, where)
        groups["row", e, i, t] = g

    def column_f(e, t):
        if Y == 1:
            return
        column = in_f.at[e, t, rows_at(halo + p.y * (Z * hub_w), Z * hub_w)]
        g = group(hub_sems, e, 2 + p.depth, t, column, column, p.y_peers[0][1])
        for _, where in p.y_peers:
            g.push(column, column, where)
        groups["row", e, p.depth, t] = g

    def send_hub_f(e, t):
        mine = rows_at(halo + (p.y * Z + p.seat) * hub_w, hub_w)
        in_f[e, t, mine, :] = out_f[e, t, halo:, :]
        if Z == 1:
            column_f(e, t)
        elif e == 0:
            pair_f(e, t, 0)
        else:
            some = in_f.at[e, t, pl.ds(halo, (Z - 1) * hub_w)]
            g = group(hub_sems, e, 2, t, some, some, p.z_peers[0][1])
            for _, where in p.z_peers:
                g.push(out_f.at[e, t, pl.ds(halo, hub_w)], in_f.at[e, t, mine], where)
            groups["row", e, 0, t] = g

    def turn_f(e, t, j):
        if j >= p.depth:
            return
        groups["row", e, j, t].wait_recv()
        if e == 0 and j + 1 < p.depth:
            pair_f(e, t, j + 1)
        else:
            column_f(e, t)

    def take_f(e, t):
        if D > 1:
            groups["halo", e, 1, t].wait_recv()
        if Y > 1:
            groups["row", e, p.depth, t].wait_recv()
        return nn(far_ref[...], in_f[e, t])

    def rest_f(e):
        for j in range(1, max(p.depth, 1)):
            for t in range(steps):
                turn_f(e, t, j)

    def put_b(e, t, field):
        value = nn(far_t_ref[...], field)
        out_b[e, t] = value.astype(BF16)
        hub_b[t] = value[halo:]

    def segment(number, base, rows):
        refs = (
            grads_ref,
            core_in,
            kept,
            square_out,
            square_in,
            z_in,
            result_ref,
            seg_send,
            seg_recv,
        )
        return Segment(p, number, base * chans, rows * chans, refs, trail)

    conv_segs = [segment(i, 2 * i, 2) for i in range(2)]
    per_kind = len(conv_segs) // 2
    mix_seg, last_seg = segment(4, 4, 2), segment(5, 6, 1)
    if chans_fit:
        refs = (grads_ref, lane_in, lane_kept, lane_out, lane_land, result_ref, seg_send, seg_recv)
        last_seg = Direct(p, 5, 6 * chans, chans, refs, trail)

    for t in range(steps):
        back = nt(cot_ref[t], mix_ref[2]).astype(BF16)
        back_ref[t] = back
        put_b(0, t, back)
        if t == 0:
            ready()
        send_hub_b(0, t)
        send_halo(0, 0, t)

    wide_ref[...] = sig_ref[...].reshape(nodes, (steps + 1) * chans)
    for kind in range(2):
        for tap in range(2):
            taps_ref[span[tap], span[kind]] = conv_ref[kind, tap]
    edge = nn(gather_ref[...], wide_ref[...]).astype(BF16)
    for t in range(steps):
        both = nn(edge[:, pair[t]], taps_ref[...])
        out_f[0, t] = (jnp.tanh(both[:, :chans]) * jax.nn.sigmoid(both[:, chans:])).astype(BF16)
        send_hub_f(0, t)

    def convolve(t):
        both = nn(wide_ref[:, pair[t]], taps_ref[...])
        tanh_filt = jnp.tanh(both[:, :chans])
        sig_gate = jax.nn.sigmoid(both[:, chans:])
        hidden_ref[t] = (tanh_filt * sig_gate).astype(BF16)
        slope_filt[t] = sig_gate * (1.0 - tanh_filt * tanh_filt)
        slope_gate[t] = tanh_filt * sig_gate * (1.0 - sig_gate)

    for t in range(steps):
        back_sum[t] = nt(cot_ref[t], mix_ref[1]) + nn(own_t_ref[...], back_ref[t])
    for t in range(steps):
        turn_b(0, t)
    for t in range(steps):
        send_halo(0, 1, t)
    for t in range(steps):
        convolve(t)
    for t in range(steps):
        turn_f(0, t, 0)

    for t in range(steps):
        back = (back_sum[t] + take_b(0, t)).astype(BF16)
        back_one_ref[t] = back
        put_b(1, t, back)
        send_hub_b(1, t)
        send_halo(1, 0, t)
    for t in range(steps):
        hop_sum[t] = nn(own_ref[...], hidden_ref[t])
    rest_f(0)
    for t in range(steps):
        back_sum[t] = nt(cot_ref[t], mix_ref[0]) + nn(own_t_ref[...], back_one_ref[t])
    for t in range(steps):
        turn_b(1, t)
    for t in range(steps):
        cot_t_ref[t] = cot_ref[t].T

    for t in range(steps):
        hop = (hop_sum[t] + take_f(0, t)).astype(BF16)
        hop_ref[t] = hop
        out_f[1, t] = nn(gather_ref[...], hop).astype(BF16)
        send_hub_f(1, t)
    for t in range(steps):
        send_halo(1, 1, t)
    for spot, field in enumerate((hidden_ref, hop_ref)):
        part = nn(cot_t_ref[0], field[0])
        for t in range(1, steps):
            part += nn(cot_t_ref[t], field[t])
        grads_ref[(4 + spot) * chans : (5 + spot) * chans, :] = part.T
    mix_seg.core_send()
    wide_t_ref[...] = wide_ref[...].T
    mix_seg.core_take()
    for t in range(steps):
        grad_hidden = back_sum[t] + take_b(1, t)
        for kind, slope in enumerate((slope_filt, slope_gate)):
            held = (grad_hidden * slope[t]).astype(BF16)
            held_ref[t, :, span[kind]] = held
            part = nn(wide_t_ref[pair[t], :], held)
            rows = slice(kind * 2 * chans, (kind + 1) * 2 * chans)
            grads_ref[rows, :] = part if t == 0 else grads_ref[rows, :] + part
            if t == steps - 1:
                for seg in conv_segs[kind * per_kind : (kind + 1) * per_kind]:
                    seg.core_send()
    for t in range(steps):
        hop_sum[t] = nn(own_ref[...], hop_ref[t])
    for seg in conv_segs:
        seg.core_take()
    for t in range(steps):
        turn_f(1, t, 0)
    mix_seg.square_take()
    for t in range(steps):
        layer_sum[t] = (
            wide_ref[:, span[t + 1]].astype(F32)
            + nn(hidden_ref[t], mix_ref[0])
            + nn(hop_ref[t], mix_ref[1])
        )
    for seg in conv_segs:
        seg.square_take()

    part = None
    for t in range(steps):
        hop = (hop_sum[t] + take_f(1, t)).astype(BF16)
        hop_ref[t] = hop
        here = nn(cot_t_ref[t], hop)
        part = here if part is None else part + here
    grads_ref[6 * chans :, :] = part.T
    last_seg.core_send()
    last_seg.core_take()
    for t in range(steps):
        layer_ref[t] = (layer_sum[t] + nn(hop_ref[t], mix_ref[2])).astype(BF16)
    carried = None
    for t in range(steps):
        into = nt(held_ref[t], taps_ref[...])
        before = into[:, :chans]
        if t > 0:
            before = before + carried
        sgrad_wide[:, span[t]] = before.astype(BF16)
        carried = into[:, chans:] + cot_ref[t].astype(F32)
    sgrad_wide[:, span[steps]] = carried.astype(BF16)
    sgrad_ref[...] = sgrad_wide[...].reshape(sgrad_ref.shape)
    mix_seg.line_take(factor)
    last_seg.square_take()
    for seg in conv_segs:
        seg.line_take(factor)
    last_seg.line_take(factor)
    for seg in (mix_seg, *conv_segs, last_seg):
        seg.spread_take()
    for seg in (mix_seg, *conv_segs, last_seg):
        seg.finish()
    for g in trail:
        g.wait_send()


def finish_kernel(layer_ref, sgrad_ref, result_ref, layer_out, sgrad_out, conv_out, mix_out, sems):
    copies = [
        pltpu.make_async_copy(layer_ref, layer_out, sems.at[0]),
        pltpu.make_async_copy(sgrad_ref, sgrad_out, sems.at[1]),
    ]
    for copy in copies:
        copy.start()
    rows = conv_out.shape[0]
    conv_out[...] = result_ref[:rows, :].astype(F32)
    mix_out[...] = result_ref[rows:, :].astype(F32)
    for copy in copies:
        copy.wait()


def shape_of(*dims, dtype=BF16):
    return jax.ShapeDtypeStruct(dims, dtype)


def room_for(scratch):
    sizes = (
        math.prod(part.shape) * jnp.dtype(part.dtype).itemsize
        for part in scratch
        if part.memory_space == pltpu.VMEM
    )
    return min(sum(sizes) + (10 << 20), 60 * 1024 * 1024)


def body(
    axis_sizes,
    signal,
    cotangent,
    conv_weight,
    mix_weight,
    send_rows,
    send_mask,
    tile_vals,
    tile_row,
    tile_col,
    tile_mask,
    hub_owner,
    hub_rows,
):
    nodes, b_dev, hist, chans = signal.shape
    steps = hist - 1
    n_dom, cap = send_rows.shape
    n_batch = dict(axis_sizes)["batch"]
    outer, inner = halves(n_dom)
    square = halves(n_batch)[0] * inner
    pair = halves(n_batch)[1]
    hub_per = hub_rows.shape[1]
    hw, hub_w = padded(cap), padded(hub_per)
    halo = n_dom * hw
    slots = halo + n_dom * hub_w
    back_rows = halo + outer * hub_w
    lead_rows = halo + hub_w
    block = tile_vals.shape[1]
    entries = n_dom * cap + hub_rows.size
    all_tiles = (nodes + entries) // block

    sig = signal.reshape(nodes, hist, chans)
    cot = jnp.transpose(cotangent.reshape(nodes, steps, chans), (1, 0, 2))

    parts = [part[None] for part in (tile_row, tile_col, tile_mask, hub_owner)]
    parts += [send_rows, send_mask, hub_rows]
    most = max(part.shape[1] for part in parts)
    table = jnp.concatenate(
        [jnp.pad(part, ((0, 0), (0, most - part.shape[1]))) for part in parts]
    )
    mats = pl.pallas_call(
        functools.partial(build_kernel, outer, inner, n_dom, hub_w, cap, hub_per),
        out_shape=(
            shape_of(nodes, nodes),
            shape_of(nodes, nodes),
            shape_of(nodes, slots),
            shape_of(slots, nodes),
            shape_of(lead_rows, nodes),
            shape_of(nodes, back_rows),
        ),
        in_specs=[HBM] * 2,
        out_specs=(VMEM,) * 6,
        scratch_shapes=[
            pltpu.VMEM((all_tiles, nodes, block), F32),
            pltpu.VMEM((entries, slots), BF16),
            pltpu.SMEM(table.shape, jnp.int32),
            pltpu.VMEM(table.shape, jnp.int32),
            pltpu.VMEM(tile_vals.shape, BF16),
            pltpu.SemaphoreType.DMA((3,)),
        ],
        compiler_params=pltpu.CompilerParams(vmem_limit_bytes=BUILD_ROOM),
        cost_estimate=pl.CostEstimate(flops=3 * 10**9, bytes_accessed=10**7, transcendentals=0),
        name="build",
    )(
        table,
        tile_vals,
    )

    total_count = nodes * steps * b_dev
    for _, size in axis_sizes:
        total_count *= size
    weights = 7 * chans
    field = pltpu.VMEM((steps, nodes, chans), BF16)
    total = pltpu.VMEM((steps, nodes, chans), F32)
    wide = pltpu.VMEM((nodes, hist * chans), BF16)
    halo_sems = pltpu.SemaphoreType.DMA((2, 2, steps))
    hub_sems = pltpu.SemaphoreType.DMA((2, 2 + outer.bit_length(), steps))
    seg_sems = pltpu.SemaphoreType.DMA((6, 5))
    lanes = [pltpu.VMEM((chans, chans // pair), kind) for kind in (F32, F32, BF16, BF16)]
    scratch = [
        wide,
        pltpu.VMEM((hist * chans, nodes), BF16),
        pltpu.VMEM((steps, chans, nodes), BF16),
        pltpu.VMEM((2 * chans, 2 * chans), BF16),
        field,
        field,
        field,
        field,
        total,
        total,
        total,
        total,
        total,
        pltpu.VMEM((steps, nodes, 2 * chans), BF16),
        wide,
        pltpu.VMEM((weights, chans), F32),
        pltpu.VMEM((2, steps, slots, chans), BF16),
        pltpu.VMEM((steps, n_dom * hub_w, chans), F32),
        pltpu.VMEM((2, steps, outer * hub_w, chans), BF16),
        pltpu.VMEM((2, steps, outer * hub_w, chans), BF16),
        pltpu.VMEM((2, steps, back_rows, chans), BF16),
        pltpu.VMEM((2, steps, lead_rows, chans), BF16),
        pltpu.VMEM((2, steps, slots, chans), BF16),
        pltpu.VMEM((weights // pair, chans), F32),
        pltpu.VMEM((weights // pair, chans), F32),
        pltpu.VMEM((square, weights // (pair * square), chans), BF16),
        pltpu.VMEM((square, weights // (pair * square), chans), BF16),
        pltpu.VMEM((outer, weights // (pair * square), chans), BF16),
        *lanes,
        halo_sems,
        halo_sems,
        hub_sems,
        hub_sems,
        seg_sems,
        seg_sems,
    ]
    layer, sgrad, result = pl.pallas_call(
        functools.partial(
            main_kernel, n_dom, n_batch, hub_w, 1.0 / math.sqrt(total_count)
        ),
        out_shape=(
            shape_of(steps, nodes, chans),
            shape_of(nodes, hist, chans),
            shape_of(weights, chans),
        ),
        in_specs=[VMEM] * 10,
        out_specs=(VMEM,) * 3,
        scratch_shapes=scratch,
        compiler_params=pltpu.CompilerParams(
            collective_id=0, has_side_effects=True, vmem_limit_bytes=room_for(scratch)
        ),
        name="main",
    )(sig, cot, conv_weight, mix_weight, *mats)

    layer_out, signal_grad, conv_grad, mix_grad = pl.pallas_call(
        finish_kernel,
        out_shape=(
            shape_of(steps, nodes, chans),
            shape_of(nodes, hist, chans),
            shape_of(4 * chans, chans, dtype=F32),
            shape_of(3 * chans, chans, dtype=F32),
        ),
        in_specs=[VMEM] * 3,
        out_specs=(ANY, ANY, VMEM, VMEM),
        scratch_shapes=[pltpu.SemaphoreType.DMA((2,))],
        compiler_params=pltpu.CompilerParams(vmem_limit_bytes=12 << 20),
        name="finish",
    )(layer, sgrad, result)
    return (
        jnp.transpose(layer_out, (1, 0, 2)).reshape(nodes, b_dev, steps, chans),
        signal_grad.reshape(signal.shape),
        conv_grad.reshape(conv_weight.shape),
        mix_grad.reshape(mix_weight.shape),
    )


def solution(mesh):
    placed = (
        P("dom", "batch", None, None),
        P("dom", "batch", None, None),
        P(),
        P(),
        P("dom", None),
        P("dom", None),
        P("dom", None, None),
        P("dom"),
        P("dom"),
        P("dom"),
        P(),
        P(),
    )
    axis_sizes = tuple((axis, mesh.shape[axis]) for axis in ("dom", "batch"))
    return jax.shard_map(
        functools.partial(body, axis_sizes),
        mesh=mesh,
        in_specs=placed,
        out_specs=(P("dom", "batch", None, None), P("dom", "batch", None, None), P(), P()),
        check_vma=False,
    )
```

```python
import functools
import math

import jax
import jax.numpy as jnp
from jax import lax
from jax.experimental import pallas as pl
from jax.experimental.pallas import tpu as pltpu
from jax.sharding import PartitionSpec as P

VMEM = pl.BlockSpec(memory_space=pltpu.VMEM)
ANY = pl.BlockSpec(memory_space=pl.ANY)
HBM = pl.BlockSpec(memory_space=pltpu.HBM)
MESH = pl.DeviceIdType.MESH
BUILD_ROOM = 52 << 20
F32 = jnp.float32
BF16 = jnp.bfloat16


def nn(left, right):
    return lax.dot_general(left, right, (((1,), (0,)), ((), ())), preferred_element_type=F32)


def nt(left, right):
    return lax.dot_general(left, right, (((1,), (1,)), ((), ())), preferred_element_type=F32)


def halves(size):
    return (size // 2, 2) if size % 2 == 0 else (size, 1)


def flipped(index, size):
    total, low, high = 0, 1, size // 2
    while high >= 1:
        total = total + lax.rem(lax.div(index, low), 2) * high
        low, high = low * 2, high // 2
    return total


def padded(rows):
    return -(-rows // 16) * 16


def build_kernel(
    outer,
    inner,
    n_dom,
    hub_width,
    cap,
    hub_per,
    table_any,
    tile_any,
    own_ref,
    own_t_ref,
    far_ref,
    far_t_ref,
    gather_ref,
    scatter_ref,
    dense_ref,
    place_ref,
    ints_ref,
    table_ref,
    tile_ref,
    sems,
):
    loads = [
        pltpu.make_async_copy(source, target, sems.at[i])
        for i, (source, target) in enumerate(
            (
                (table_any, ints_ref),
                (table_any, table_ref),
                (tile_any, tile_ref),
            )
        )
    ]
    for load in loads:
        load.start()
    nodes = own_ref.shape[0]
    tiles, block, _ = tile_ref.shape
    own_tiles = nodes // block
    all_tiles = dense_ref.shape[0]
    slots = far_ref.shape[1]
    groups = ints_ref.shape[0] - 4 - 2 * n_dom
    rows_ref, flag_ref = table_ref.at[4 : 4 + n_dom], table_ref.at[4 + n_dom : 4 + 2 * n_dom]
    hubs_ref = table_ref.at[4 + 2 * n_dom :]
    halo_slots = gather_ref.shape[0] - hub_width
    halo_width = halo_slots // n_dom
    halo = n_dom * cap

    dense_ref[...] = jnp.zeros_like(dense_ref)
    entry = lax.broadcasted_iota(jnp.int32, (halo, slots), 0)
    if cap != halo_width:
        entry = lax.div(entry, cap) * halo_width + lax.rem(entry, cap)
    place_ref[:halo, :] = jnp.where(
        entry == lax.broadcasted_iota(jnp.int32, (halo, slots), 1), 1.0, 0.0
    ).astype(BF16)
    source = lax.div(lax.broadcasted_iota(jnp.int32, (halo_slots, n_dom), 0), halo_width)
    expand = (source == lax.broadcasted_iota(jnp.int32, (halo_slots, n_dom), 1)).astype(F32)
    lane = lax.rem(lax.broadcasted_iota(jnp.int32, (halo_slots, cap), 0), halo_width)
    for load in loads[:-1]:
        load.wait()
    slot = lax.broadcasted_iota(jnp.int32, (hub_per, slots), 1)
    entry = lax.broadcasted_iota(jnp.int32, (hub_per, slots), 0) + halo_slots
    me = lax.axis_index("dom")
    hub = jnp.zeros((1, hub_per), F32)
    for o in range(groups):
        at = halo + o * hub_per
        owner = ints_ref[3, o]
        seat = lax.rem(owner, inner) * outer + flipped(lax.div(owner, inner), outer)
        place_ref[at : at + hub_per, :] = jnp.where(
            slot == entry + seat * hub_width, 1.0, 0.0
        ).astype(BF16)
        owned = (owner == me).astype(F32)
        hub += owned * (hubs_ref[o : o + 1, :hub_per].astype(F32) + 1.0)
    chosen = jnp.where(flag_ref[:, :cap] == 1, rows_ref[:, :cap].astype(F32) + 1.0, 0.0)
    spread = jnp.dot(
        expand, chosen, precision=lax.Precision.HIGHEST, preferred_element_type=F32
    )
    from_halo = jnp.where(
        lax.broadcasted_iota(jnp.int32, (halo_slots, cap), 1) == lane, spread, 0.0
    )
    from_hub = jnp.where(
        lax.broadcasted_iota(jnp.int32, (hub_width, hub_per), 1)
        == lax.broadcasted_iota(jnp.int32, (hub_width, hub_per), 0),
        jnp.broadcast_to(hub, (hub_width, hub_per)),
        0.0,
    )

    def picked(values):
        pick = (jnp.sum(values, axis=1, keepdims=True) + 0.5).astype(jnp.int32) - 1
        node = lax.broadcasted_iota(jnp.int32, (values.shape[0], nodes), 1)
        return jnp.where(pick == node, 1.0, 0.0)

    halo_pick, hub_pick = picked(from_halo), picked(from_hub)
    gather_ref[:halo_slots, :] = halo_pick.astype(BF16)
    gather_ref[halo_slots:, :] = hub_pick.astype(BF16)
    scatter_ref[...] = (
        jnp.concatenate([halo_pick] + [hub_pick] * outer, axis=0).T.astype(BF16)
    )
    loads[-1].wait()
    for t in range(tiles):

        @pl.when(ints_ref[2, t] == 1)
        def _():
            rows = pl.ds(pl.multiple_of(ints_ref[0, t] * block, block), block)
            dense_ref[ints_ref[1, t], rows, :] += tile_ref[t].astype(F32)

    far = nn(dense_ref[own_tiles].astype(BF16), place_ref[:block, :])
    for c in range(own_tiles + 1, all_tiles):
        at = (c - own_tiles) * block
        far += nn(dense_ref[c].astype(BF16), place_ref[at : at + block, :])
    far_ref[...] = far.astype(BF16)
    far_t_ref[...] = far.T.astype(BF16)
    for c in range(own_tiles):
        part = dense_ref[c]
        own_ref[:, c * block : (c + 1) * block] = part.astype(BF16)
        own_t_ref[c * block : (c + 1) * block, :] = part.T.astype(BF16)


def rows_at(start, count):
    return pl.ds(pl.multiple_of(start, 16), count)


class Group:
    def __init__(self, trail, send_sem, recv_sem, sent, landed, where):
        self.send_sem, self.recv_sem = send_sem, recv_sem
        self.sent, self.landed, self.where = sent, landed, where
        trail.append(self)

    def push(self, source, target, where):
        pltpu.make_async_remote_copy(
            src_ref=source,
            dst_ref=target,
            send_sem=self.send_sem,
            recv_sem=self.recv_sem,
            device_id=where,
            device_id_type=MESH,
        ).start()

    def whole(self):
        return pltpu.make_async_remote_copy(
            src_ref=self.sent,
            dst_ref=self.landed,
            send_sem=self.send_sem,
            recv_sem=self.recv_sem,
            device_id=self.where,
            device_id_type=MESH,
        )

    def wait_recv(self):
        self.whole().wait_recv()

    def wait_send(self):
        self.whole().wait_send()


class Segment:
    def __init__(self, place, number, base, rows, refs, trail):
        self.p, self.n, self.base, self.rows, self.trail = place, number, base, rows, trail
        (self.grads, self.core_in, self.kept, self.out, self.inn, self.z_in, self.result) = refs[:7]
        self.send_sem, self.recv_sem = refs[7:]
        p = place
        self.half = rows // p.K
        self.piece = self.half // len(p.square)
        self.half_at = base // p.K
        self.piece_at = base // (p.K * len(p.square))
        self.mine = base + p.k * self.half + p.g * self.piece
        self.small = pl.ds(self.piece_at, self.piece)

    def group(self, stage, sent, landed, where):
        return Group(
            self.trail,
            self.send_sem.at[self.n, stage],
            self.recv_sem.at[self.n, stage],
            sent,
            landed,
            where,
        )

    def core_send(self):
        p = self.p
        if p.K == 1:
            return
        spot = self.core_in.at[pl.ds(self.half_at, self.half)]
        self.core = self.group(0, spot, spot, p.partner)
        give = self.base + p.other_k * self.half
        self.core.push(self.grads.at[rows_at(give, self.half)], spot, p.partner)

    def core_take(self):
        p = self.p
        value = self.grads[rows_at(self.base + p.k * self.half, self.half), :]
        if p.K > 1:
            self.core.wait_recv()
            value = value + self.core_in[pl.ds(self.half_at, self.half), :]
        self.kept[pl.ds(self.half_at, self.half), :] = value
        count = len(p.square)
        for g in range(count):
            self.out[g, self.small, :] = value[g * self.piece : (g + 1) * self.piece].astype(BF16)
        if count > 1:
            some = self.inn.at[pl.ds(0, count - 1), self.small]
            self.square = self.group(1, some, some, p.square_peers[0][1])
            for other, where in p.square_peers:
                self.square.push(
                    self.out.at[other, self.small], self.inn.at[p.g, self.small], where
                )

    def square_take(self):
        p = self.p
        value = self.kept[rows_at(self.half_at + p.g * self.piece, self.piece), :]
        if len(p.square) > 1:
            self.square.wait_recv()
            for other, _ in p.square_peers:
                value = value + self.inn[other, self.small, :].astype(F32)
        self.z_in[p.z, self.small, :] = value.astype(BF16)
        if p.Z > 1:
            some = self.z_in.at[pl.ds(0, p.Z - 1), self.small]
            self.line = self.group(2, some, some, p.z_peers[0][1])
            spot = self.z_in.at[p.z, self.small]
            for _, where in p.z_peers:
                self.line.push(spot, spot, where)

    def line_take(self, factor):
        p = self.p
        if p.Z > 1:
            self.line.wait_recv()
        value = self.z_in[0, self.small, :].astype(F32)
        for i in range(1, p.Z):
            value = value + self.z_in[i, self.small, :].astype(F32)
        spot = rows_at(self.mine, self.piece)
        self.result[spot, :] = (value * factor).astype(BF16)
        count = len(p.square)
        if count > 1:
            some = self.result.at[pl.ds(self.base, (count - 1) * self.piece)]
            self.spread = self.group(3, some, some, p.square_peers[0][1])
            for _, where in p.square_peers:
                self.spread.push(self.result.at[spot], self.result.at[spot], where)

    def spread_take(self):
        p = self.p
        if len(p.square) > 1:
            self.spread.wait_recv()
        if p.K > 1:
            spot = self.result.at[rows_at(self.base + p.k * self.half, self.half)]
            self.last = self.group(4, spot, spot, p.partner)
            self.last.push(spot, spot, p.partner)

    def finish(self):
        if self.p.K > 1:
            self.last.wait_recv()


class Direct:
    def __init__(self, place, number, base, rows, refs, trail):
        self.p, self.base, self.rows, self.trail = place, base, rows, trail
        self.grads, self.core_in, self.kept, self.out, self.inn, self.result = refs[:6]
        self.send_sem, self.recv_sem = refs[6].at[number], refs[7].at[number]
        self.lanes = self.grads.shape[1] // place.K
        self.piece = rows // len(place.chips)
        self.half = pl.ds(pl.multiple_of(place.k * self.lanes, 128), self.lanes)
        self.mine = rows_at(base + place.c * self.piece, self.piece)

    def group(self, stage, sent, landed, where):
        return Group(
            self.trail, self.send_sem.at[stage], self.recv_sem.at[stage], sent, landed, where
        )

    def core_send(self):
        p = self.p
        if p.K == 1:
            return
        other = pl.ds(pl.multiple_of(p.other_k * self.lanes, 128), self.lanes)
        self.core = self.group(0, self.core_in, self.core_in, p.partner)
        self.core.push(
            self.grads.at[pl.ds(self.base, self.rows), other], self.core_in, p.partner
        )

    def core_take(self):
        p = self.p
        value = self.grads[pl.ds(self.base, self.rows), self.half]
        if p.K > 1:
            self.core.wait_recv()
            value = value + self.core_in[...]
        self.kept[...] = value
        self.out[...] = value.astype(BF16)
        count = len(p.chips)
        if count > 1:
            some = self.inn.at[pl.ds(0, (count - 1) * self.piece)]
            self.chip = self.group(1, some, some, p.chip_peers[0][1])
            for other, where in p.chip_peers:
                self.chip.push(
                    self.out.at[rows_at(other * self.piece, self.piece)],
                    self.inn.at[rows_at(p.c * self.piece, self.piece)],
                    where,
                )

    def chip_take(self, factor):
        p = self.p
        value = self.kept[rows_at(p.c * self.piece, self.piece), :]
        if len(p.chips) > 1:
            self.chip.wait_recv()
            for other, _ in p.chip_peers:
                value = value + self.inn[rows_at(other * self.piece, self.piece), :].astype(F32)
        self.result[self.mine, self.half] = (value * factor).astype(BF16)
        if len(p.chips) > 1:
            rows = pl.ds(self.base, (len(p.chips) - 1) * self.piece)
            some = self.result.at[rows, self.half]
            self.spread = self.group(3, some, some, p.chip_peers[0][1])
            spot = self.result.at[self.mine, self.half]
            for _, where in p.chip_peers:
                self.spread.push(spot, spot, where)

    def square_take(self):
        pass

    def line_take(self, factor):
        self.chip_take(factor)

    def spread_take(self):
        p = self.p
        if len(p.chips) > 1:
            self.spread.wait_recv()
        if p.K > 1:
            spot = self.result.at[pl.ds(self.base, self.rows), self.half]
            self.last = self.group(4, spot, spot, p.partner)
            self.last.push(spot, spot, p.partner)

    def finish(self):
        if self.p.K > 1:
            self.last.wait_recv()


def direct_fits(chips, cores, chans):
    return chans % (chips * 16) == 0 and chans % (cores * 128) == 0


class Place:
    def __init__(self, n_dom, n_batch):
        self.D = n_dom
        self.Z, self.Y = halves(n_dom)
        self.X, self.K = halves(n_batch)
        self.me = lax.axis_index("dom")
        batch = lax.axis_index("batch")
        self.z, self.y = lax.div(self.me, self.Y), lax.rem(self.me, self.Y)
        self.x, self.k = lax.div(batch, self.K), lax.rem(batch, self.K)
        self.other_k = lax.rem(self.k + 1, self.K)
        self.partner = {"batch": self.x * self.K + self.other_k}
        self.dom_peers = [lax.rem(self.me + d, n_dom) for d in range(1, n_dom)]
        self.z_peers = []
        for d in range(1, self.Z):
            seat = lax.rem(self.z + d, self.Z)
            self.z_peers.append((seat, {"dom": seat * self.Y + self.y}))
        self.y_peers = []
        for d in range(1, self.Y):
            seat = lax.rem(self.y + d, self.Y)
            self.y_peers.append((seat, {"dom": self.z * self.Y + seat}))
        assert self.Z & (self.Z - 1) == 0
        self.seat = flipped(self.z, self.Z)
        self.depth = self.Z.bit_length() - 1
        self.z_pairs = []
        for i in range(self.depth):
            stride = self.Z >> (i + 1)
            other = self.z + stride - 2 * stride * lax.rem(lax.div(self.z, stride), 2)
            kept = self.seat - lax.rem(self.seat, 1 << i)
            given = kept + (1 << i) - 2 * (1 << i) * lax.rem(lax.div(kept, 1 << i), 2)
            self.z_pairs.append((kept, given, {"dom": other * self.Y + self.y}))
        self.square = range(self.X * self.Y)
        self.g = self.x * self.Y + self.y
        self.square_peers = []
        for d in range(1, self.X * self.Y):
            seat = lax.rem(self.g + d, self.X * self.Y)
            where = {
                "batch": lax.div(seat, self.Y) * self.K + self.k,
                "dom": self.z * self.Y + lax.rem(seat, self.Y),
            }
            self.square_peers.append((seat, where))

        self.chips = range(n_dom * self.X)
        self.c = self.me * self.X + self.x
        self.chip_peers = []
        for d in range(1, n_dom * self.X):
            seat = lax.rem(self.c + d, n_dom * self.X)
            where = {
                "dom": lax.div(seat, self.X),
                "batch": lax.rem(seat, self.X) * self.K + self.k,
            }
            self.chip_peers.append((seat, where))

    def greet(self, everyone):
        barrier = pltpu.get_barrier_semaphore()
        if everyone:
            peers = [where for _, where in self.chip_peers]
        else:
            peers = [{"dom": other} for other in self.dom_peers] + self.across()
        if self.K > 1:
            peers.append(self.partner)
        for where in peers:
            pl.semaphore_signal(barrier, inc=1, device_id=where, device_id_type=MESH)
        return lambda: pl.semaphore_wait(barrier, len(peers))

    def across(self):
        peers = []
        for x in range(1, self.X):
            for y in range(self.Y):
                peers.append(
                    {
                        "batch": lax.rem(self.x + x, self.X) * self.K + self.k,
                        "dom": self.z * self.Y + lax.rem(self.y + y, self.Y),
                    }
                )
        return peers


def main_kernel(
    n_dom,
    n_batch,
    hub_w,
    factor,
    sig_ref,
    cot_ref,
    conv_ref,
    mix_ref,
    own_ref,
    own_t_ref,
    far_ref,
    far_t_ref,
    gather_ref,
    scatter_ref,
    layer_ref,
    sgrad_ref,
    result_ref,
    wide_ref,
    wide_t_ref,
    cot_t_ref,
    taps_ref,
    hidden_ref,
    hop_ref,
    back_ref,
    back_one_ref,
    slope_filt,
    slope_gate,
    hop_sum,
    back_sum,
    layer_sum,
    held_ref,
    sgrad_wide,
    grads_ref,
    out_b,
    hub_b,
    hub_in,
    hub_out,
    in_b,
    out_f,
    in_f,
    core_in,
    kept,
    square_out,
    square_in,
    z_in,
    lane_in,
    lane_kept,
    lane_out,
    lane_land,
    halo_send,
    halo_recv,
    hub_send,
    hub_recv,
    seg_send,
    seg_recv,
):
    steps, nodes, chans = cot_ref.shape
    p = Place(n_dom, n_batch)
    D, Z, Y = p.D, p.Z, p.Y
    chans_fit = direct_fits(len(p.chips), p.K, chans)
    ready = p.greet(chans_fit)
    halo = gather_ref.shape[0] - hub_w
    hw = halo // D
    trail = []
    span = [slice(t * chans, (t + 1) * chans) for t in range(steps + 1)]
    pair = [slice(t * chans, (t + 2) * chans) for t in range(steps)]

    def group(sems, e, kind, t, sent, landed, where):
        return Group(
            trail, sems[0].at[e, kind, t], sems[1].at[e, kind, t], sent, landed, where
        )

    halo_sems, hub_sems = (halo_send, halo_recv), (hub_send, hub_recv)
    groups = {}

    def send_halo(e, kind, t):
        out, inn = (out_b, in_b) if kind == 0 else (out_f, in_f)
        some = inn.at[e, t, pl.ds(0, (D - 1) * hw)]
        g = group(halo_sems, e, kind, t, some, some, {"dom": p.dom_peers[0]})
        mine = rows_at(p.me * hw, hw)
        for other in p.dom_peers:
            g.push(
                out.at[e, t, rows_at(other * hw, hw)], inn.at[e, t, mine], {"dom": other}
            )
        groups["halo", e, kind, t] = g
        inn[e, t, mine, :] = out[e, t, mine, :]

    def send_hub_b(e, t):
        if Y == 1:
            return
        g = group(hub_sems, e, 0, t, hub_in.at[e, t], hub_in.at[e, t], p.y_peers[0][1])
        for seat, where in p.y_peers:
            g.push(
                out_b.at[e, t, rows_at(halo + seat * (Z * hub_w), Z * hub_w)],
                hub_in.at[e, t],
                where,
            )
        groups["hub", e, 0, t] = g

    def turn_b(e, t):
        value = hub_b[t, rows_at(p.y * (Z * hub_w), Z * hub_w), :]
        if Y > 1:
            groups["hub", e, 0, t].wait_recv()
            value = value + hub_in[e, t].astype(F32)
        hub_out[e, t] = value.astype(BF16)
        mine = rows_at(halo + p.z * hub_w, hub_w)
        if Z > 1:
            some = in_b.at[e, t, pl.ds(halo, (Z - 1) * hub_w)]
            g = group(hub_sems, e, 1, t, some, some, p.z_peers[0][1])
            for seat, where in p.z_peers:
                g.push(
                    hub_out.at[e, t, rows_at(flipped(seat, Z) * hub_w, hub_w)],
                    in_b.at[e, t, mine],
                    where,
                )
            groups["hub", e, 1, t] = g
        in_b[e, t, mine, :] = hub_out[e, t, rows_at(p.seat * hub_w, hub_w), :]

    def take_b(e, t):
        if D > 1:
            groups["halo", e, 0, t].wait_recv()
        if Z > 1:
            groups["hub", e, 1, t].wait_recv()
        return nn(scatter_ref[...], in_b[e, t])

    def pair_f(e, t, i):
        kept, given, where = p.z_pairs[i]
        base, count = halo + p.y * (Z * hub_w), hub_w << i
        land = in_f.at[e, t, rows_at(base + given * hub_w, count)]
        spot = in_f.at[e, t, rows_at(base + kept * hub_w, count)]
        source = out_f.at[e, t, pl.ds(halo, hub_w)] if i == 0 else spot
        g = group(hub_sems, e, 2 + i, t, land, land, where)
        g.push(source, spot, where)
        groups["row", e, i, t] = g

    def column_f(e, t):
        if Y == 1:
            return
        column = in_f.at[e, t, rows_at(halo + p.y * (Z * hub_w), Z * hub_w)]
        g = group(hub_sems, e, 2 + p.depth, t, column, column, p.y_peers[0][1])
        for _, where in p.y_peers:
            g.push(column, column, where)
        groups["row", e, p.depth, t] = g

    def send_hub_f(e, t):
        mine = rows_at(halo + (p.y * Z + p.seat) * hub_w, hub_w)
        in_f[e, t, mine, :] = out_f[e, t, halo:, :]
        if Z == 1:
            column_f(e, t)
        elif e == 0:
            pair_f(e, t, 0)
        else:
            some = in_f.at[e, t, pl.ds(halo, (Z - 1) * hub_w)]
            g = group(hub_sems, e, 2, t, some, some, p.z_peers[0][1])
            for _, where in p.z_peers:
                g.push(out_f.at[e, t, pl.ds(halo, hub_w)], in_f.at[e, t, mine], where)
            groups["row", e, 0, t] = g

    def turn_f(e, t, j):
        if j >= p.depth:
            return
        groups["row", e, j, t].wait_recv()
        if e == 0 and j + 1 < p.depth:
            pair_f(e, t, j + 1)
        else:
            column_f(e, t)

    def take_f(e, t):
        if D > 1:
            groups["halo", e, 1, t].wait_recv()
        if Y > 1:
            groups["row", e, p.depth, t].wait_recv()
        return nn(far_ref[...], in_f[e, t])

    def rest_f(e):
        for j in range(1, max(p.depth, 1)):
            for t in range(steps):
                turn_f(e, t, j)

    def put_b(e, t, field):
        value = nn(far_t_ref[...], field)
        out_b[e, t] = value.astype(BF16)
        hub_b[t] = value[halo:]

    def segment(number, base, rows):
        refs = (
            grads_ref,
            core_in,
            kept,
            square_out,
            square_in,
            z_in,
            result_ref,
            seg_send,
            seg_recv,
        )
        return Segment(p, number, base * chans, rows * chans, refs, trail)

    conv_segs = [segment(i, 2 * i, 2) for i in range(2)]
    per_kind = len(conv_segs) // 2
    mix_seg, last_seg = segment(4, 4, 2), segment(5, 6, 1)
    if chans_fit:
        refs = (grads_ref, lane_in, lane_kept, lane_out, lane_land, result_ref, seg_send, seg_recv)
        last_seg = Direct(p, 5, 6 * chans, chans, refs, trail)

    for t in range(steps):
        back = nt(cot_ref[t], mix_ref[2]).astype(BF16)
        back_ref[t] = back
        put_b(0, t, back)
        if t == 0:
            ready()
        send_hub_b(0, t)
        send_halo(0, 0, t)

    wide_ref[...] = sig_ref[...].reshape(nodes, (steps + 1) * chans)
    for kind in range(2):
        for tap in range(2):
            taps_ref[span[tap], span[kind]] = conv_ref[kind, tap]
    edge = nn(gather_ref[...], wide_ref[...]).astype(BF16)
    for t in range(steps):
        both = nn(edge[:, pair[t]], taps_ref[...])
        out_f[0, t] = (jnp.tanh(both[:, :chans]) * jax.nn.sigmoid(both[:, chans:])).astype(BF16)
        send_hub_f(0, t)

    def convolve(t):
        both = nn(wide_ref[:, pair[t]], taps_ref[...])
        tanh_filt = jnp.tanh(both[:, :chans])
        sig_gate = jax.nn.sigmoid(both[:, chans:])
        hidden_ref[t] = (tanh_filt * sig_gate).astype(BF16)
        slope_filt[t] = sig_gate * (1.0 - tanh_filt * tanh_filt)
        slope_gate[t] = tanh_filt * sig_gate * (1.0 - sig_gate)

    for t in range(steps):
        back_sum[t] = nt(cot_ref[t], mix_ref[1]) + nn(own_t_ref[...], back_ref[t])
    for t in range(steps):
        turn_b(0, t)
    for t in range(steps):
        send_halo(0, 1, t)
    for t in range(steps):
        convolve(t)
    for t in range(steps):
        turn_f(0, t, 0)

    for t in range(steps):
        back = (back_sum[t] + take_b(0, t)).astype(BF16)
        back_one_ref[t] = back
        put_b(1, t, back)
        send_hub_b(1, t)
    for t in range(steps):
        send_halo(1, 0, t)
    for t in range(steps):
        hop_sum[t] = nn(own_ref[...], hidden_ref[t])
    rest_f(0)
    for t in range(steps):
        back_sum[t] = nt(cot_ref[t], mix_ref[0]) + nn(own_t_ref[...], back_one_ref[t])
    for t in range(steps):
        turn_b(1, t)
    for t in range(steps):
        cot_t_ref[t] = cot_ref[t].T

    for t in range(steps):
        hop = (hop_sum[t] + take_f(0, t)).astype(BF16)
        hop_ref[t] = hop
        out_f[1, t] = nn(gather_ref[...], hop).astype(BF16)
        send_hub_f(1, t)
    for t in range(steps):
        send_halo(1, 1, t)
    for spot, field in enumerate((hidden_ref, hop_ref)):
        part = nn(cot_t_ref[0], field[0])
        for t in range(1, steps):
            part += nn(cot_t_ref[t], field[t])
        grads_ref[(4 + spot) * chans : (5 + spot) * chans, :] = part.T
    mix_seg.core_send()
    wide_t_ref[...] = wide_ref[...].T
    mix_seg.core_take()
    for t in range(steps):
        grad_hidden = back_sum[t] + take_b(1, t)
        for kind, slope in enumerate((slope_filt, slope_gate)):
            held = (grad_hidden * slope[t]).astype(BF16)
            held_ref[t, :, span[kind]] = held
            part = nn(wide_t_ref[pair[t], :], held)
            rows = slice(kind * 2 * chans, (kind + 1) * 2 * chans)
            grads_ref[rows, :] = part if t == 0 else grads_ref[rows, :] + part
            if t == steps - 1:
                for seg in conv_segs[kind * per_kind : (kind + 1) * per_kind]:
                    seg.core_send()
    for t in range(steps):
        hop_sum[t] = nn(own_ref[...], hop_ref[t])
    for seg in conv_segs:
        seg.core_take()
    for t in range(steps):
        turn_f(1, t, 0)
    mix_seg.square_take()
    for t in range(steps):
        layer_sum[t] = (
            wide_ref[:, span[t + 1]].astype(F32)
            + nn(hidden_ref[t], mix_ref[0])
            + nn(hop_ref[t], mix_ref[1])
        )
    for seg in conv_segs:
        seg.square_take()

    part = None
    for t in range(steps):
        hop = (hop_sum[t] + take_f(1, t)).astype(BF16)
        hop_ref[t] = hop
        here = nn(cot_t_ref[t], hop)
        part = here if part is None else part + here
    grads_ref[6 * chans :, :] = part.T
    last_seg.core_send()
    last_seg.core_take()
    for t in range(steps):
        layer_ref[t] = (layer_sum[t] + nn(hop_ref[t], mix_ref[2])).astype(BF16)
    carried = None
    for t in range(steps):
        into = nt(held_ref[t], taps_ref[...])
        before = into[:, :chans]
        if t > 0:
            before = before + carried
        sgrad_wide[:, span[t]] = before.astype(BF16)
        carried = into[:, chans:] + cot_ref[t].astype(F32)
    sgrad_wide[:, span[steps]] = carried.astype(BF16)
    sgrad_ref[...] = sgrad_wide[...].reshape(sgrad_ref.shape)
    last_seg.square_take()
    for seg in (*conv_segs, mix_seg, last_seg):
        seg.line_take(factor)
    for seg in (*conv_segs, mix_seg, last_seg):
        seg.spread_take()
    for seg in (mix_seg, *conv_segs, last_seg):
        seg.finish()
    for g in trail:
        g.wait_send()


def finish_kernel(
    layer_ref, sgrad_ref, result_ref, layer_out, sgrad_out, conv_out, mix_out, stage, sems
):
    chans = result_ref.shape[1]
    copies = []

    def send(source, target):
        copy = pltpu.make_async_copy(source, target, sems.at[len(copies)])
        copy.start()
        copies.append(copy)

    send(layer_ref, layer_out)
    send(sgrad_ref, sgrad_out)
    for base, out in ((0, conv_out), (conv_out.shape[0], mix_out)):
        for at in range(0, out.shape[0], chans):
            rows = pl.ds(base + at, chans)
            stage[rows, :] = result_ref[rows, :].astype(F32)
            send(stage.at[rows], out.at[pl.ds(at, chans)])
    for copy in copies:
        copy.wait()


def shape_of(*dims, dtype=BF16):
    return jax.ShapeDtypeStruct(dims, dtype)


def room_for(scratch):
    sizes = (
        math.prod(part.shape) * jnp.dtype(part.dtype).itemsize
        for part in scratch
        if part.memory_space == pltpu.VMEM
    )
    return min(sum(sizes) + (10 << 20), 60 * 1024 * 1024)


def body(
    axis_sizes,
    signal,
    cotangent,
    conv_weight,
    mix_weight,
    send_rows,
    send_mask,
    tile_vals,
    tile_row,
    tile_col,
    tile_mask,
    hub_owner,
    hub_rows,
):
    nodes, b_dev, hist, chans = signal.shape
    steps = hist - 1
    n_dom, cap = send_rows.shape
    n_batch = dict(axis_sizes)["batch"]
    outer, inner = halves(n_dom)
    square = halves(n_batch)[0] * inner
    pair = halves(n_batch)[1]
    hub_per = hub_rows.shape[1]
    hw, hub_w = padded(cap), padded(hub_per)
    halo = n_dom * hw
    slots = halo + n_dom * hub_w
    back_rows = halo + outer * hub_w
    lead_rows = halo + hub_w
    block = tile_vals.shape[1]
    entries = n_dom * cap + hub_rows.size
    all_tiles = (nodes + entries) // block

    sig = signal.reshape(nodes, hist, chans)
    cot = jnp.transpose(cotangent.reshape(nodes, steps, chans), (1, 0, 2))

    parts = [part[None] for part in (tile_row, tile_col, tile_mask, hub_owner)]
    parts += [send_rows, send_mask, hub_rows]
    most = max(part.shape[1] for part in parts)
    table = jnp.concatenate(
        [jnp.pad(part, ((0, 0), (0, most - part.shape[1]))) for part in parts]
    )
    mats = pl.pallas_call(
        functools.partial(build_kernel, outer, inner, n_dom, hub_w, cap, hub_per),
        out_shape=(
            shape_of(nodes, nodes),
            shape_of(nodes, nodes),
            shape_of(nodes, slots),
            shape_of(slots, nodes),
            shape_of(lead_rows, nodes),
            shape_of(nodes, back_rows),
        ),
        in_specs=[HBM] * 2,
        out_specs=(VMEM,) * 6,
        scratch_shapes=[
            pltpu.VMEM((all_tiles, nodes, block), F32),
            pltpu.VMEM((entries, slots), BF16),
            pltpu.SMEM(table.shape, jnp.int32),
            pltpu.VMEM(table.shape, jnp.int32),
            pltpu.VMEM(tile_vals.shape, BF16),
            pltpu.SemaphoreType.DMA((3,)),
        ],
        compiler_params=pltpu.CompilerParams(vmem_limit_bytes=BUILD_ROOM),
        cost_estimate=pl.CostEstimate(flops=3 * 10**9, bytes_accessed=10**7, transcendentals=0),
        name="build",
    )(
        table,
        tile_vals,
    )

    total_count = nodes * steps * b_dev
    for _, size in axis_sizes:
        total_count *= size
    weights = 7 * chans
    field = pltpu.VMEM((steps, nodes, chans), BF16)
    total = pltpu.VMEM((steps, nodes, chans), F32)
    wide = pltpu.VMEM((nodes, hist * chans), BF16)
    halo_sems = pltpu.SemaphoreType.DMA((2, 2, steps))
    hub_sems = pltpu.SemaphoreType.DMA((2, 2 + outer.bit_length(), steps))
    seg_sems = pltpu.SemaphoreType.DMA((6, 5))
    lanes = [pltpu.VMEM((chans, chans // pair), kind) for kind in (F32, F32, BF16, BF16)]
    scratch = [
        wide,
        pltpu.VMEM((hist * chans, nodes), BF16),
        pltpu.VMEM((steps, chans, nodes), BF16),
        pltpu.VMEM((2 * chans, 2 * chans), BF16),
        field,
        field,
        field,
        field,
        total,
        total,
        total,
        total,
        total,
        pltpu.VMEM((steps, nodes, 2 * chans), BF16),
        wide,
        pltpu.VMEM((weights, chans), F32),
        pltpu.VMEM((2, steps, slots, chans), BF16),
        pltpu.VMEM((steps, n_dom * hub_w, chans), F32),
        pltpu.VMEM((2, steps, outer * hub_w, chans), BF16),
        pltpu.VMEM((2, steps, outer * hub_w, chans), BF16),
        pltpu.VMEM((2, steps, back_rows, chans), BF16),
        pltpu.VMEM((2, steps, lead_rows, chans), BF16),
        pltpu.VMEM((2, steps, slots, chans), BF16),
        pltpu.VMEM((weights // pair, chans), F32),
        pltpu.VMEM((weights // pair, chans), F32),
        pltpu.VMEM((square, weights // (pair * square), chans), BF16),
        pltpu.VMEM((square, weights // (pair * square), chans), BF16),
        pltpu.VMEM((outer, weights // (pair * square), chans), BF16),
        *lanes,
        halo_sems,
        halo_sems,
        hub_sems,
        hub_sems,
        seg_sems,
        seg_sems,
    ]
    layer, sgrad, result = pl.pallas_call(
        functools.partial(
            main_kernel, n_dom, n_batch, hub_w, 1.0 / math.sqrt(total_count)
        ),
        out_shape=(
            shape_of(steps, nodes, chans),
            shape_of(nodes, hist, chans),
            shape_of(weights, chans),
        ),
        in_specs=[VMEM] * 10,
        out_specs=(VMEM,) * 3,
        scratch_shapes=scratch,
        compiler_params=pltpu.CompilerParams(
            collective_id=0, has_side_effects=True, vmem_limit_bytes=room_for(scratch)
        ),
        name="main",
    )(sig, cot, conv_weight, mix_weight, *mats)

    layer_out, signal_grad, conv_grad, mix_grad = pl.pallas_call(
        finish_kernel,
        out_shape=(
            shape_of(steps, nodes, chans),
            shape_of(nodes, hist, chans),
            shape_of(4 * chans, chans, dtype=F32),
            shape_of(3 * chans, chans, dtype=F32),
        ),
        in_specs=[VMEM] * 3,
        out_specs=(ANY,) * 4,
        scratch_shapes=[pltpu.VMEM((weights, chans), F32), pltpu.SemaphoreType.DMA((9,))],
        compiler_params=pltpu.CompilerParams(vmem_limit_bytes=12 << 20),
        name="finish",
    )(layer, sgrad, result)
    return (
        jnp.transpose(layer_out, (1, 0, 2)).reshape(nodes, b_dev, steps, chans),
        signal_grad.reshape(signal.shape),
        conv_grad.reshape(conv_weight.shape),
        mix_grad.reshape(mix_weight.shape),
    )


def solution(mesh):
    placed = (
        P("dom", "batch", None, None),
        P("dom", "batch", None, None),
        P(),
        P(),
        P("dom", None),
        P("dom", None),
        P("dom", None, None),
        P("dom"),
        P("dom"),
        P("dom"),
        P(),
        P(),
    )
    axis_sizes = tuple((axis, mesh.shape[axis]) for axis in ("dom", "batch"))
    return jax.shard_map(
        functools.partial(body, axis_sizes),
        mesh=mesh,
        in_specs=placed,
        out_specs=(P("dom", "batch", None, None), P("dom", "batch", None, None), P(), P()),
        check_vma=False,
    )
```
